128 devices in a mesh: ba: 16 (over x_lo, y, core), col: 8 (over x_hi, z).
Axes of the slice: x: 4 (x_hi: 2, x_lo: 2; x = x_hi * 2 + x_lo), y: 4, z: 4, core: 2. Of those that a mesh axis runs over, the one named last changes fastest.
Arguments:
- r_pairs: bfloat16 [1, 3, 512, 512], replicated, may hold values from -6 to 6
- w_tiles: bfloat16 [1, 3, 512, 512, 512], P(None, None, 'ba', 'col'), may hold values from -0.375 to 0.375
- virt_energy: float32 [512], replicated, may hold values from 0.3 to 3
- energy_shift: float32 [1], replicated, may hold values from -14 to -8
Outputs:
- sigma: float32 [1, 3, 512, 512], P(None, None, 'ba', 'col')
The draws below stay inside these ranges and needn't reach their ends.
All inputs are finite; a program needn't handle non-finite values.
Results may differ from the reference program's by a relative error of at most 0.00077.
Values may be sent and summed in bfloat16 or wider, within the bound.
No kernel may reach another device: no remote copies, remote signals or barrier semaphores. Data moves between devices by JAX's collectives and lax.ppermute only.
A program may use at most 64 MiB of HBM per device.

```python
import jax
import jax.numpy as jnp
from jax import lax

V = 512
TRIPLES = 1


def spiked(drawn, own_key, source, target, blocks, factor):
    owner, partner = [(jnp.arange(drawn.shape[dim]) // (drawn.shape[dim] // blocks)).reshape([-1 if axis == dim else 1 for axis in range(drawn.ndim)]) for dim in (source, target)]
    chosen = jax.random.permutation(own_key, blocks)[partner]
    strong = (owner == chosen) | (owner == (partner + blocks // 2) % blocks)
    return jnp.where(strong, factor * drawn, drawn)


def levels(key, extent, shards, smallest, top_value):
    factor_of, own = 1.0, jax.random.fold_in(key, 6)
    for position, parts in shards:
        steps = jnp.exp(jax.random.uniform(jax.random.fold_in(own, position), (parts,), jnp.float32, smallest / len(shards), top_value / len(shards)))
        factor_of = factor_of * jnp.repeat(steps, extent[position] // parts).reshape([-1 if axis == position else 1 for axis in range(len(extent))])
    return factor_of


def noise(stream_key, dims, deviation, most, shards=(), kind=jnp.bfloat16):
    drawn = deviation * jax.random.normal(stream_key, dims, jnp.float32)
    if shards:
        drawn = drawn * levels(stream_key, dims, shards, -0.22, 0.18)
    return jnp.clip(drawn, -most, most).astype(kind)


def heavy_noise(stream_key, extent, scale, reach, shards, heavy, dtype=jnp.bfloat16):
    result = scale * jax.random.normal(stream_key, extent, jnp.float32)
    if shards:
        result = result * levels(stream_key, extent, shards, -0.22, 0.18)
    return jnp.clip(spiked(result, jax.random.fold_in(stream_key, 3), *heavy), -reach, reach).astype(dtype)


def setup_inputs(seed: int = 0) -> dict:
    key_list = jax.random.split(jax.random.key(seed), 5)
    return {
        "r_pairs": noise(key_list[0], (TRIPLES, 3, V, V), 1.0, 6.0),
        "w_tiles": heavy_noise(key_list[1], (TRIPLES, 3, V, V, V), V ** -0.5, 0.375, ((2, 16), (3, 8)), (3, 4, 8, 2.0)),
        "virt_energy": jnp.clip(jax.random.uniform(key_list[2], (V,), jnp.float32, 0.3, 3.0), 0.3, 3.0),
        "energy_shift": jnp.clip(jax.random.uniform(key_list[3], (TRIPLES,), jnp.float32, -14.0, -8.0), -14.0, -8.0),
    }


def one_triple(inputs):
    rows, tiles, shift_value = inputs
    flat = tiles.reshape(3, V * V, V)
    cubes = jnp.dot(rows[0], flat[0].T, preferred_element_type=jnp.float32)
    cubes = cubes + jnp.dot(rows[1], flat[1].T, preferred_element_type=jnp.float32)
    cubes = cubes + jnp.dot(rows[2], flat[2].T, preferred_element_type=jnp.float32)
    cubes = cubes.astype(jnp.bfloat16).reshape(V, V, V)
    bc_summed = (cubes.astype(jnp.float32) + jnp.swapaxes(cubes, 1, 2).astype(jnp.float32)).astype(jnp.bfloat16)
    return bc_summed, flat, shift_value


def reference(r_pairs, w_tiles, virt_energy, energy_shift):
    def finish(inputs):
        bc_summed, flat, shift_value = one_triple(inputs)
        combined = bc_summed.astype(jnp.float32) + jnp.swapaxes(bc_summed, 0, 1).astype(jnp.float32)
        denominator = shift_value - virt_energy[:, None, None] - virt_energy[None, :, None] - virt_energy[None, None, :]
        combined = (combined / denominator).astype(jnp.bfloat16).reshape(V, V * V)
        blocks = [jnp.dot(combined, flat[which], preferred_element_type=jnp.float32) for which in range(3)]
        return jnp.stack(blocks)

    return lax.map(finish, (r_pairs, w_tiles, energy_shift))
```

```python
import jax
import jax.numpy as jnp
from jax import lax
from jax.experimental import pallas as pl
from jax.experimental.pallas import tpu as pltpu
from jax.sharding import PartitionSpec as P

F32 = jnp.float32
BF16 = jnp.bfloat16
VMEM_LIMIT = 56 * 1024 * 1024


def cube_kernel(r_ref, w_ref, out_ref):
    acc = None
    for m in range(3):
        rows = w_ref[m].reshape(512, 512)
        term = lax.dot_general(
            r_ref[m], rows, (((1,), (1,)), ((), ())), preferred_element_type=F32
        )
        acc = term if acc is None else acc + term
    out_ref[...] = acc.astype(BF16).reshape(16, 1, 32, 512)


def make_cubes(r_pairs, w):
    return pl.pallas_call(
        cube_kernel,
        grid=(2, 2),
        in_specs=[
            pl.BlockSpec((3, 512, 512), lambda h, s: (0, 0, 0)),
            pl.BlockSpec((3, 16, 32, 512), lambda h, s: (0, s, h, 0)),
        ],
        out_specs=pl.BlockSpec((16, 1, 32, 512), lambda h, s: (0, h, 0, s)),
        out_shape=jax.ShapeDtypeStruct((16, 2, 32, 1024), BF16),
        compiler_params=pltpu.CompilerParams(vmem_limit_bytes=VMEM_LIMIT),
        name="cubes",
    )(r_pairs, w)


def group_select(lane, bit, low, high):
    keep = (lane & bit) == 0
    first = jnp.where(keep, low, pltpu.roll(high, bit, 1))
    second = jnp.where(keep, pltpu.roll(low, 128 - bit, 1), high)
    return first, second


def combine_kernel(
    x_ref, u1_ref, u2_ref, u3_ref, perm_ref, ea_ref, eb_ref, ec_ref, w_ref, out_ref,
    stage_ref, swap_ref, comb_ref,
):
    perm = perm_ref[...]
    lane = lax.broadcasted_iota(jnp.int32, (8, 128), 1)
    eb = eb_ref[...]
    for k in range(4):
        u2 = jnp.dot(u2_ref[k].reshape(64, 1024), perm, preferred_element_type=F32)
        u3 = jnp.dot(u3_ref[k].reshape(64, 1024), perm, preferred_element_type=F32)
        shifted = ea_ref[k]
        for h in range(2):
            other = u1_ref[k, h].astype(F32) + u2[32 * h : 32 * h + 32]
            other = other.astype(BF16).astype(F32)
            for j in range(8):
                stage_ref[j] = other[:, 128 * j : 128 * j + 128]
            for j in range(8):
                g = [stage_ref[:, 4 * j + f, :] for f in range(4)]
                m0, m2 = group_select(lane, 64, g[0], g[2])
                m1, m3 = group_select(lane, 64, g[1], g[3])
                d0, d1 = group_select(lane, 32, m0, m1)
                d2, d3 = group_select(lane, 32, m2, m3)
                for e, d in enumerate((d0, d1, d2, d3)):
                    swap_ref[j, pl.ds(e, 8, stride=4), :] = d
            own = x_ref[k, h].astype(F32) + u3[32 * h : 32 * h + 32]
            own = own.astype(BF16).astype(F32)
            swapped = jnp.concatenate([swap_ref[j] for j in range(8)], axis=1)
            den = (shifted - eb) - ec_ref[h : h + 1]
            comb = ((own + swapped) / den).astype(BF16)
            comb_ref[32 * k : 32 * k + 32, 1024 * h : 1024 * h + 1024] = comb
    low = lax.broadcasted_iota(jnp.int32, (16, 128), 1) < 64
    for m in range(3):
        sig = None
        for h in range(2):
            rows = w_ref[m, :, 32 * h : 32 * h + 32, :].reshape(1024, 512)
            term = jnp.dot(
                comb_ref[:, 1024 * h : 1024 * h + 1024], rows, preferred_element_type=F32
            )
            sig = term if sig is None else sig + term
        for k in range(4):
            for t in range(4):
                top = sig[32 * k : 32 * k + 16, 128 * t : 128 * t + 128]
                bottom = sig[32 * k + 16 : 32 * k + 32, 128 * t : 128 * t + 128]
                even = jnp.where(low, top, pltpu.roll(bottom, 64, 1))
                odd = jnp.where(low, pltpu.roll(top, 64, 1), bottom)
                out_ref[k, 2 * t, 16 * m : 16 * m + 16, :] = even.astype(BF16)
                out_ref[k, 2 * t + 1, 16 * m : 16 * m + 16, :] = odd.astype(BF16)


def combine(x, u1, u2, u3, perm, ea, eb, ec, w):
    blocks = pl.BlockSpec((4, 2, 32, 1024), lambda s: (s, 0, 0, 0))

    def whole(shape):
        return pl.BlockSpec(shape, lambda s: (0,) * len(shape), pipeline_mode=pl.Buffered(1))

    return pl.pallas_call(
        combine_kernel,
        grid=(4,),
        in_specs=[
            blocks, blocks, blocks, blocks,
            whole((1024, 1024)),
            pl.BlockSpec((4, 32, 1), lambda s: (s, 0, 0)),
            whole((1, 1024)),
            whole((2, 1024)),
            whole((3, 32, 64, 512)),
        ],
        out_specs=pl.BlockSpec((4, 8, 48, 128), lambda s: (s, 0, 0, 0)),
        out_shape=jax.ShapeDtypeStruct((16, 8, 48, 128), BF16),
        scratch_shapes=[
            pltpu.VMEM((8, 32, 128), F32),
            pltpu.VMEM((8, 32, 128), F32),
            pltpu.VMEM((128, 2048), BF16),
        ],
        compiler_params=pltpu.CompilerParams(vmem_limit_bytes=VMEM_LIMIT),
        name="combine",
    )(x, u1, u2, u3, perm, ea, eb, ec, w)


def total_kernel(parts_ref, out_ref):
    total = parts_ref[0:8].astype(F32).sum(axis=0)
    for s in range(1, 16):
        total = total + parts_ref[8 * s : 8 * s + 8].astype(F32).sum(axis=0)
    for m in range(3):
        out_ref[m, 0:16, :] = total[16 * m : 16 * m + 16, 0:64]
        out_ref[m, 16:32, :] = total[16 * m : 16 * m + 16, 64:128]


def total_of(parts):
    return pl.pallas_call(
        total_kernel,
        out_shape=jax.ShapeDtypeStruct((3, 32, 64), F32),
        compiler_params=pltpu.CompilerParams(vmem_limit_bytes=VMEM_LIMIT),
        name="total",
    )(parts)


def exchange(x, axis):
    return lax.all_to_all(x, axis, split_axis=0, concat_axis=0, tiled=True)


def on_device(r_pairs, w_tiles, virt_energy, energy_shift):
    w = w_tiles[0]
    x = make_cubes(r_pairs[0], w)
    u1 = exchange(x, "ba")
    u2 = exchange(u1.reshape(8, 2, 2, 32, 1024), "col")
    u2 = jnp.swapaxes(u2, 1, 2).reshape(16, 2, 32, 1024)
    u3 = exchange(u2, "ba")
    perm = jnp.arange(1024)
    perm = ((perm % 32) * 32 + perm // 32)[:, None] == perm[None, :]
    b_start = lax.axis_index("ba") * 32
    c_start = lax.axis_index("col") * 64
    energy_b = lax.dynamic_slice_in_dim(virt_energy, b_start, 32)
    energy_c = lax.dynamic_slice_in_dim(virt_energy, c_start, 64)
    ea = (energy_shift - virt_energy).reshape(16, 32, 1)
    eb = jnp.broadcast_to(energy_b[:, None], (32, 32)).reshape(1, 1024)
    ec = jnp.broadcast_to(energy_c.reshape(2, 1, 32), (2, 32, 32)).reshape(2, 1024)
    parts = combine(x, u1, u2, u3, perm.astype(BF16), ea, eb, ec, w)
    arrived = exchange(parts.reshape(128, 48, 128), ("ba", "col"))
    return total_of(arrived)[None]


def solution(mesh):
    in_specs = (P(), P(None, None, "ba", "col", None), P(), P())
    out_specs = P(None, None, "ba", "col")
    return jax.shard_map(
        on_device, mesh=mesh, in_specs=in_specs, out_specs=out_specs, check_vma=False
    )
```

```python
import jax
import jax.numpy as jnp
from jax import lax
from jax.experimental import pallas as pl
from jax.experimental.pallas import tpu as pltpu
from jax.sharding import PartitionSpec as P

F32 = jnp.float32
BF16 = jnp.bfloat16
VMEM_LIMIT = 56 * 1024 * 1024


def cube_kernel(r_ref, w_ref, out_ref):
    acc = None
    for m in range(3):
        rows = w_ref[m].reshape(512, 512)
        term = lax.dot_general(
            r_ref[m], rows, (((1,), (1,)), ((), ())), preferred_element_type=F32
        )
        acc = term if acc is None else acc + term
    out_ref[...] = acc.astype(BF16).reshape(16, 1, 32, 512)


def make_cubes(r_pairs, w):
    return pl.pallas_call(
        cube_kernel,
        grid=(2, 2),
        in_specs=[
            pl.BlockSpec((3, 512, 512), lambda h, s: (0, 0, 0)),
            pl.BlockSpec((3, 16, 32, 512), lambda h, s: (0, s, h, 0)),
        ],
        out_specs=pl.BlockSpec((16, 1, 32, 512), lambda h, s: (0, h, 0, s)),
        out_shape=jax.ShapeDtypeStruct((16, 2, 32, 1024), BF16),
        compiler_params=pltpu.CompilerParams(vmem_limit_bytes=VMEM_LIMIT),
        name="cubes",
    )(r_pairs, w)


def group_select(lane, bit, low, high):
    keep = (lane & bit) == 0
    first = jnp.where(keep, low, pltpu.roll(high, bit, 1))
    second = jnp.where(keep, pltpu.roll(low, 128 - bit, 1), high)
    return first, second


def swap_kernel(u1_ref, u2_ref, perm_ref, out_ref, stage_ref, swap_ref):
    lane = lax.broadcasted_iota(jnp.int32, (8, 128), 1)
    u2 = jnp.dot(u2_ref[...].reshape(256, 1024), perm_ref[...], preferred_element_type=F32)
    for k in range(4):
        for h in range(2):
            row = 64 * k + 32 * h
            other = u1_ref[k, h].astype(F32) + u2[row : row + 32]
            for j in range(8):
                stage_ref[j] = other[:, 128 * j : 128 * j + 128]
            for j in range(8):
                g = [stage_ref[:, 4 * j + f, :] for f in range(4)]
                m0, m2 = group_select(lane, 64, g[0], g[2])
                m1, m3 = group_select(lane, 64, g[1], g[3])
                d0, d1 = group_select(lane, 32, m0, m1)
                d2, d3 = group_select(lane, 32, m2, m3)
                for e, d in enumerate((d0, d1, d2, d3)):
                    swap_ref[j, pl.ds(e, 8, stride=4), :] = d
            for j in range(8):
                out_ref[k, h, :, 128 * j : 128 * j + 128] = swap_ref[j].astype(BF16)


def whole(shape):
    return pl.BlockSpec(shape, lambda s: (0,) * len(shape), pipeline_mode=pl.Buffered(1))


def swapped_sum(u1, u2, perm):
    blocks = pl.BlockSpec((4, 2, 32, 1024), lambda s: (s, 0, 0, 0))
    return pl.pallas_call(
        swap_kernel,
        grid=(4,),
        in_specs=[blocks, blocks, whole((1024, 1024))],
        out_specs=blocks,
        out_shape=jax.ShapeDtypeStruct((16, 2, 32, 1024), BF16),
        scratch_shapes=[pltpu.VMEM((8, 32, 128), F32), pltpu.VMEM((8, 32, 128), F32)],
        compiler_params=pltpu.CompilerParams(vmem_limit_bytes=16 * 1024 * 1024),
        cost_estimate=pl.CostEstimate(
            flops=2 * 1024**3, bytes_accessed=10 * 1024**2, transcendentals=0
        ),
        name="swapped_sum",
    )(u1, u2, perm)


def combine_kernel(x_ref, u3_ref, swapped_ref, perm_ref, ea_ref, eb_ref, ec_ref, w_ref, out_ref, comb_ref):
    step = pl.program_id(0)
    u3 = jnp.dot(u3_ref[...].reshape(256, 1024), perm_ref[...], preferred_element_type=F32)
    eb = eb_ref[...]
    for k in range(4):
        shifted = ea_ref[k]
        for h in range(2):
            row = 64 * k + 32 * h
            own = (x_ref[k, h].astype(F32) + u3[row : row + 32]).astype(BF16).astype(F32)
            den = (shifted - eb) - ec_ref[h : h + 1]
            comb = ((own + swapped_ref[k, h].astype(F32)) / den).astype(BF16)
            comb_ref[step, 32 * k : 32 * k + 32, 1024 * h : 1024 * h + 1024] = comb

    @pl.when(step == 3)
    def _():
        low = lax.broadcasted_iota(jnp.int32, (16, 128), 1) < 64
        for m in range(3):
            sig = None
            for h in range(2):
                rows = w_ref[m, :, 32 * h : 32 * h + 32, :].reshape(1024, 512)
                left = comb_ref[:, :, 1024 * h : 1024 * h + 1024].reshape(512, 1024)
                term = jnp.dot(left, rows, preferred_element_type=F32)
                sig = term if sig is None else sig + term
            for k in range(16):
                for t in range(4):
                    top = sig[32 * k : 32 * k + 16, 128 * t : 128 * t + 128]
                    bottom = sig[32 * k + 16 : 32 * k + 32, 128 * t : 128 * t + 128]
                    even = jnp.where(low, top, pltpu.roll(bottom, 64, 1))
                    odd = jnp.where(low, pltpu.roll(top, 64, 1), bottom)
                    out_ref[k, 2 * t, 16 * m : 16 * m + 16, :] = even.astype(BF16)
                    out_ref[k, 2 * t + 1, 16 * m : 16 * m + 16, :] = odd.astype(BF16)


def combine(x, u3, swapped, perm, ea, eb, ec, w):
    blocks = pl.BlockSpec((4, 2, 32, 1024), lambda s: (s, 0, 0, 0))
    return pl.pallas_call(
        combine_kernel,
        grid=(4,),
        in_specs=[
            blocks, blocks, blocks,
            whole((1024, 1024)),
            pl.BlockSpec((4, 32, 1), lambda s: (s, 0, 0)),
            whole((1, 1024)),
            whole((2, 1024)),
            whole((3, 32, 64, 512)),
        ],
        out_specs=whole((16, 8, 48, 128)),
        out_shape=jax.ShapeDtypeStruct((16, 8, 48, 128), BF16),
        scratch_shapes=[pltpu.VMEM((4, 128, 2048), BF16)],
        compiler_params=pltpu.CompilerParams(vmem_limit_bytes=VMEM_LIMIT),
        name="combine",
    )(x, u3, swapped, perm, ea, eb, ec, w)


def total_kernel(parts_ref, out_ref):
    total = parts_ref[0:8].astype(F32).sum(axis=0)
    for s in range(1, 16):
        total = total + parts_ref[8 * s : 8 * s + 8].astype(F32).sum(axis=0)
    for m in range(3):
        out_ref[m, 0:16, :] = total[16 * m : 16 * m + 16, 0:64]
        out_ref[m, 16:32, :] = total[16 * m : 16 * m + 16, 64:128]


def total_of(parts):
    return pl.pallas_call(
        total_kernel,
        out_shape=jax.ShapeDtypeStruct((3, 32, 64), F32),
        compiler_params=pltpu.CompilerParams(vmem_limit_bytes=VMEM_LIMIT),
        name="total",
    )(parts)


def exchange(x, axis):
    return lax.all_to_all(x, axis, split_axis=0, concat_axis=0, tiled=True)


def on_device(r_pairs, w_tiles, virt_energy, energy_shift):
    w = w_tiles[0]
    x = make_cubes(r_pairs[0], w)
    u1 = exchange(x, "ba")
    u2 = exchange(u1.reshape(8, 2, 2, 32, 1024), "col")
    u2 = jnp.swapaxes(u2, 1, 2).reshape(16, 2, 32, 1024)
    u3 = exchange(u2, "ba")
    perm = jnp.arange(1024)
    perm = (((perm % 32) * 32 + perm // 32)[:, None] == perm[None, :]).astype(BF16)
    b_start = lax.axis_index("ba") * 32
    c_start = lax.axis_index("col") * 64
    energy_b = lax.dynamic_slice_in_dim(virt_energy, b_start, 32)
    energy_c = lax.dynamic_slice_in_dim(virt_energy, c_start, 64)
    ea = (energy_shift - virt_energy).reshape(16, 32, 1)
    eb = jnp.broadcast_to(energy_b[:, None], (32, 32)).reshape(1, 1024)
    ec = jnp.broadcast_to(energy_c.reshape(2, 1, 32), (2, 32, 32)).reshape(2, 1024)
    swapped = swapped_sum(u1, u2, perm)
    parts = combine(x, u3, swapped, perm, ea, eb, ec, w)
    arrived = exchange(parts.reshape(128, 48, 128), ("ba", "col"))
    return total_of(arrived)[None]


def solution(mesh):
    in_specs = (P(), P(None, None, "ba", "col", None), P(), P())
    out_specs = P(None, None, "ba", "col")
    return jax.shard_map(
        on_device, mesh=mesh, in_specs=in_specs, out_specs=out_specs, check_vma=False
    )
```

```python
import jax
import jax.numpy as jnp
from jax import lax
from jax.experimental import pallas as pl
from jax.experimental.pallas import tpu as pltpu
from jax.sharding import PartitionSpec as P

F32 = jnp.float32
BF16 = jnp.bfloat16
VMEM_LIMIT = 56 * 1024 * 1024


def lane_bits(g):
    lane = lax.broadcasted_iota(jnp.int32, (8, 128), 1)
    value = ((lane >> 2) & 7) ^ g
    return [((value >> t) & 1) == 1 for t in range(3)]


def butterfly(values, masks):
    for t, mask in enumerate(masks):
        bit = 1 << t
        values = [jnp.where(mask, values[k ^ bit], values[k]) for k in range(len(values))]
    return values


def halves(first, second, top):
    return (
        jnp.where(top, first, pltpu.roll(second, 4, 0)),
        jnp.where(top, pltpu.roll(first, 4, 0), second),
    )


def group_select(lane, bit, low, high):
    keep = (lane & bit) == 0
    first = jnp.where(keep, low, pltpu.roll(high, bit, 1))
    second = jnp.where(keep, pltpu.roll(low, 128 - bit, 1), high)
    return first, second


def whole(shape):
    return pl.BlockSpec(shape, lambda s: (0,) * len(shape), pipeline_mode=pl.Buffered(1))


def params(limit=VMEM_LIMIT):
    return pltpu.CompilerParams(vmem_limit_bytes=limit)


SMEM_SPEC = pl.BlockSpec(memory_space=pltpu.SMEM)


def cube_kernel(place_ref, r_ref, w_ref, out_ref, x_ref):
    step = pl.program_id(0)
    base = place_ref[0] ^ (2 * place_ref[1])
    top = lax.broadcasted_iota(jnp.int32, (8, 128), 0) < 4
    masks = lane_bits(0)
    for half in range(2):
        acc = None
        for m in range(3):
            rows = w_ref[m, :, 32 * half : 32 * half + 32, :].reshape(256, 512)
            term = lax.dot_general(
                r_ref[m], rows, (((1,), (1,)), ((), ())), preferred_element_type=F32
            )
            acc = term if acc is None else acc + term
        x_ref[half] = acc.reshape(16, 32, 256)

    @pl.loop(0, 16)
    def _(a_hi):
        h = a_hi ^ base
        for tile in range(2):
            lanes = slice(128 * tile, 128 * tile + 128)
            values = []
            for t in range(4):
                values += halves(
                    x_ref[0, a_hi, 8 * t : 8 * t + 8, lanes],
                    x_ref[1, a_hi ^ 1, 8 * t : 8 * t + 8, lanes],
                    top,
                )
            for k, value in enumerate(butterfly(values, masks)):
                g = k ^ (2 * step + tile)
                out_ref[8 * h + g, :, lanes] = value.astype(BF16)


def make_cubes(place, r_pairs, w):
    return pl.pallas_call(
        cube_kernel,
        grid=(4,),
        in_specs=[
            SMEM_SPEC,
            whole((3, 512, 512)),
            pl.BlockSpec((3, 8, 64, 512), lambda s: (0, s, 0, 0)),
        ],
        out_specs=pl.BlockSpec((128, 8, 256), lambda s: (0, 0, s)),
        out_shape=jax.ShapeDtypeStruct((128, 8, 1024), BF16),
        scratch_shapes=[pltpu.VMEM((2, 16, 32, 256), F32)],
        compiler_params=params(),
        name="cubes",
    )(place, r_pairs, w)


def owner_bits(h, c_h):
    row = lax.broadcasted_iota(jnp.int32, (8, 128), 0)
    value = (2 * row + c_h) ^ h
    return [((value >> t) & 1) == 1 for t in range(4)]


def denominator_kernel(place_ref, ea_ref, eb_ref, ec_ref, out_ref, part_ref):
    lanes = lane_bits(place_ref[1])

    @pl.loop(0, 8)
    def _(x):
        for c_h in range(2):
            rows = owner_bits(place_ref[0], c_h)
            for a_r in range(4):
                values = [jnp.full((8, 128), ea_ref[32 * k + 4 * x + a_r], F32) for k in range(16)]
                for k, value in enumerate(butterfly(values, rows)):
                    part_ref[x, k, c_h, a_r] = value

    @pl.loop(0, 16)
    def _(k):
        for c_h in range(2):
            ec = ec_ref[c_h]
            for a_r in range(4):
                values = [part_ref[x, k, c_h, a_r] for x in range(8)]
                for x, value in enumerate(butterfly(values, lanes)):
                    out_ref[x, k, c_h, a_r] = (value - eb_ref[x, k]) - ec


def denominators(place, ea, eb, ec):
    shape = (8, 16, 2, 4, 8, 128)
    return pl.pallas_call(
        denominator_kernel,
        grid=(1,),
        in_specs=[SMEM_SPEC, SMEM_SPEC, whole((8, 16, 1, 128)), whole((2, 8, 128))],
        out_specs=whole(shape),
        out_shape=jax.ShapeDtypeStruct(shape, F32),
        scratch_shapes=[pltpu.VMEM(shape, F32)],
        compiler_params=params(24 * 1024 * 1024),
        cost_estimate=pl.CostEstimate(
            flops=20 * 1024**2, bytes_accessed=20 * 1024**2, transcendentals=0
        ),
        name="denominators",
    )(place, ea, eb, ec)


def owner_kernel(place_ref, m_ref, perm_ref, den_ref, out_ref, mf_ref, mp_ref, s_ref, q_ref):
    lane = lax.broadcasted_iota(jnp.int32, (8, 128), 1)
    lanes = lane_bits(place_ref[1])
    for part in range(4):
        block = m_ref[32 * part : 32 * part + 32].reshape(256, 1024)
        moved = jnp.dot(block, perm_ref[...], preferred_element_type=F32)
        for x in range(8):
            column = slice(128 * x, 128 * x + 128)
            mp_ref[x, 2 * part : 2 * part + 2] = moved[:, column].reshape(2, 16, 8, 128)
            mf_ref[x, 4 * part : 4 * part + 4] = (
                m_ref[32 * part : 32 * part + 32, :, column].astype(F32).reshape(4, 8, 8, 128)
            )

    @pl.loop(0, 8)
    def _(pair):
        for odd in range(2):
            i = 2 * pair + odd
            for c_h in range(2):
                summed = []
                for a_r in range(4):
                    values = []
                    for x in range(8):
                        own = mf_ref[x, i, :, 4 * c_h + a_r, :]
                        moved = mp_ref[x, :, 8 * c_h + pair, 4 * odd + a_r, :]
                        value = (own + moved).astype(BF16).astype(F32)
                        s_ref[x, i, c_h, a_r] = value
                        values.append(value)
                    summed.append(butterfly(values, lanes))
                for x in range(8):
                    m0, m2 = group_select(lane, 64, summed[0][x], summed[2][x])
                    m1, m3 = group_select(lane, 64, summed[1][x], summed[3][x])
                    d0, d1 = group_select(lane, 32, m0, m1)
                    d2, d3 = group_select(lane, 32, m2, m3)
                    for e, d in enumerate((d0, d1, d2, d3)):
                        q_ref[x, i, c_h, e] = d

    @pl.loop(0, 8)
    def _(x):
        for c_h in range(2):
            rows = owner_bits(place_ref[0], c_h)
            for a_r in range(4):
                values = butterfly([q_ref[x, i, c_h, a_r] for i in range(16)], rows)
                for i in range(16):
                    total = s_ref[x, i, c_h, a_r] + values[i]
                    mf_ref[x, i, :, 4 * c_h + a_r, :] = total / den_ref[x, i, c_h, a_r]

    for x in range(8):
        out_ref[:, :, 128 * x : 128 * x + 128] = mf_ref[x].reshape(128, 8, 128).astype(BF16)


def combine_at_owner(place, m, perm, den):
    shape = (8, 16, 2, 4, 8, 128)
    return pl.pallas_call(
        owner_kernel,
        grid=(1,),
        in_specs=[SMEM_SPEC, whole((128, 8, 1024)), whole((1024, 1024)), whole(shape)],
        out_specs=whole((128, 8, 1024)),
        out_shape=jax.ShapeDtypeStruct((128, 8, 1024), BF16),
        scratch_shapes=[
            pltpu.VMEM((8, 16, 8, 8, 128), F32),
            pltpu.VMEM((8, 8, 16, 8, 128), F32),
            pltpu.VMEM(shape, F32),
            pltpu.VMEM(shape, F32),
        ],
        compiler_params=params(),
        name="combine_at_owner",
    )(place, m, perm, den)


def contract_kernel(place_ref, m_ref, w_ref, out_ref, comb_ref, sum_ref):
    step = pl.program_id(0)
    base = place_ref[0] ^ (2 * place_ref[1])
    top = lax.broadcasted_iota(jnp.int32, (8, 128), 0) < 4
    masks = lane_bits(0)

    @pl.loop(0, 16)
    def _(a_hi):
        h = a_hi ^ base
        for tile in range(2):
            lanes = slice(128 * tile, 128 * tile + 128)
            values = []
            for k in range(8):
                g = k ^ (2 * step + tile)
                values.append(m_ref[8 * h + g, :, lanes].astype(F32))
            values = butterfly(values, masks)
            for t in range(2):
                first = halves(values[4 * t], values[4 * t + 1], top)
                second = halves(values[4 * t + 2], values[4 * t + 3], top)
                for half in range(2):
                    rows = jnp.concatenate([first[half], second[half]], axis=0).astype(BF16)
                    comb_ref[half, a_hi ^ half, 16 * t : 16 * t + 16, lanes] = rows

    for m in range(3):
        term = None
        for half in range(2):
            rows = w_ref[m, :, 32 * half : 32 * half + 32, :].reshape(256, 512)
            left = comb_ref[half].reshape(512, 256)
            product = jnp.dot(left, rows, preferred_element_type=F32)
            term = product if term is None else term + product

        @pl.when(step == 0)
        def _(m=m, term=term):
            sum_ref[m] = term

        @pl.when(step > 0)
        def _(m=m, term=term):
            sum_ref[m] = sum_ref[m] + term

    @pl.when(step == 3)
    def _():
        low = lax.broadcasted_iota(jnp.int32, (16, 128), 1) < 64
        for m in range(3):
            for k in range(16):
                for t in range(4):
                    column = slice(128 * t, 128 * t + 128)
                    upper = sum_ref[m, 32 * k : 32 * k + 16, column]
                    lower = sum_ref[m, 32 * k + 16 : 32 * k + 32, column]
                    even = jnp.where(low, upper, pltpu.roll(lower, 64, 1))
                    odd = jnp.where(low, pltpu.roll(upper, 64, 1), lower)
                    out_ref[k, 2 * t, 16 * m : 16 * m + 16, :] = even.astype(BF16)
                    out_ref[k, 2 * t + 1, 16 * m : 16 * m + 16, :] = odd.astype(BF16)


def contract(place, m, w):
    return pl.pallas_call(
        contract_kernel,
        grid=(4,),
        in_specs=[
            SMEM_SPEC,
            pl.BlockSpec((128, 8, 256), lambda s: (0, 0, s)),
            pl.BlockSpec((3, 8, 64, 512), lambda s: (0, s, 0, 0)),
        ],
        out_specs=whole((16, 8, 48, 128)),
        out_shape=jax.ShapeDtypeStruct((16, 8, 48, 128), BF16),
        scratch_shapes=[pltpu.VMEM((2, 16, 32, 256), BF16), pltpu.VMEM((3, 512, 512), F32)],
        compiler_params=params(),
        name="contract",
    )(place, m, w)


def total_kernel(parts_ref, out_ref):
    total = parts_ref[0:8].astype(F32).sum(axis=0)
    for s in range(1, 16):
        total = total + parts_ref[8 * s : 8 * s + 8].astype(F32).sum(axis=0)
    for m in range(3):
        out_ref[m, 0:16, :] = total[16 * m : 16 * m + 16, 0:64]
        out_ref[m, 16:32, :] = total[16 * m : 16 * m + 16, 64:128]


def total_of(parts):
    return pl.pallas_call(
        total_kernel,
        out_shape=jax.ShapeDtypeStruct((3, 32, 64), F32),
        compiler_params=pltpu.CompilerParams(vmem_limit_bytes=VMEM_LIMIT),
        name="total",
    )(parts)


def exchange(x, axis):
    return lax.all_to_all(x, axis, split_axis=0, concat_axis=0, tiled=True)


def on_device(r_pairs, w_tiles, virt_energy, energy_shift):
    w = w_tiles[0]
    place = jnp.stack([lax.axis_index("ba"), lax.axis_index("col")]).astype(jnp.int32)
    cubes = make_cubes(place, r_pairs[0], w)
    met = exchange(cubes, ("ba", "col"))
    ea = energy_shift - virt_energy
    eb = jnp.broadcast_to(virt_energy.reshape(16, 8, 4, 1), (16, 8, 4, 32))
    eb = jnp.swapaxes(eb.reshape(16, 8, 1, 128), 0, 1)
    ec = jnp.broadcast_to(virt_energy.reshape(8, 2, 1, 32), (8, 2, 4, 32))
    ec = jnp.swapaxes(ec.reshape(8, 2, 128), 0, 1)
    den = denominators(place, ea, eb, ec)
    perm = jnp.arange(1024)
    perm = (((perm % 32) * 32 + perm // 32)[:, None] == perm[None, :]).astype(BF16)
    combined = combine_at_owner(place, met, perm, den)
    home = exchange(combined, ("ba", "col"))
    parts = contract(place, home, w)
    arrived = exchange(parts.reshape(128, 48, 128), ("ba", "col"))
    return total_of(arrived)[None]


def solution(mesh):
    in_specs = (P(), P(None, None, "ba", "col", None), P(), P())
    out_specs = P(None, None, "ba", "col")
    return jax.shard_map(
        on_device, mesh=mesh, in_specs=in_specs, out_specs=out_specs, check_vma=False
    )
```

```python
import jax
import jax.numpy as jnp
import numpy as np
from jax import lax
from jax.experimental import pallas as pl
from jax.experimental.pallas import tpu as pltpu
from jax.sharding import PartitionSpec as P

F32 = jnp.float32
BF16 = jnp.bfloat16
VMEM_LIMIT = 24 * 1024 * 1024


def lane_bits(g):
    lane = lax.broadcasted_iota(jnp.int32, (8, 128), 1)
    value = ((lane >> 2) & 7) ^ g
    return [((value >> t) & 1) == 1 for t in range(3)]


def butterfly(values, masks):
    for t, mask in enumerate(masks):
        bit = 1 << t
        values = [jnp.where(mask, values[k ^ bit], values[k]) for k in range(len(values))]
    return values


def halves(first, second, top):
    return (
        jnp.where(top, first, pltpu.roll(second, 4, 0)),
        jnp.where(top, pltpu.roll(first, 4, 0), second),
    )


def group_select(lane, bit, low, high):
    keep = (lane & bit) == 0
    first = jnp.where(keep, low, pltpu.roll(high, bit, 1))
    second = jnp.where(keep, pltpu.roll(low, 128 - bit, 1), high)
    return first, second


def whole(shape):
    return pl.BlockSpec(shape, lambda s: (0,) * len(shape), pipeline_mode=pl.Buffered(1))


def params(limit=VMEM_LIMIT):
    return pltpu.CompilerParams(vmem_limit_bytes=limit)


SMEM_SPEC = pl.BlockSpec(memory_space=pltpu.SMEM)


def cube_kernel(r_ref, w_ref, out_ref, x_ref):
    step = pl.program_id(0)
    base = lax.axis_index("ba") ^ (2 * lax.axis_index("col"))
    top = lax.broadcasted_iota(jnp.int32, (8, 128), 0) < 4
    masks = lane_bits(0)
    for half in range(2):
        acc = None
        for m in range(3):
            rows = w_ref[m, :, 32 * half : 32 * half + 32, :].reshape(256, 512)
            term = lax.dot_general(
                r_ref[m], rows, (((1,), (1,)), ((), ())), preferred_element_type=F32
            )
            acc = term if acc is None else acc + term
        x_ref[half] = acc.reshape(16, 32, 256)

    @pl.loop(0, 16)
    def _(a_hi):
        h = a_hi ^ base
        for tile in range(2):
            lanes = slice(128 * tile, 128 * tile + 128)
            values = []
            for t in range(4):
                values += halves(
                    x_ref[0, a_hi, 8 * t : 8 * t + 8, lanes],
                    x_ref[1, a_hi ^ 1, 8 * t : 8 * t + 8, lanes],
                    top,
                )
            for k, value in enumerate(butterfly(values, masks)):
                g = k ^ (2 * step + tile)
                out_ref[8 * h + g, :, lanes] = value.astype(BF16)


def make_cubes(r_pairs, w):
    return pl.pallas_call(
        cube_kernel,
        grid=(4,),
        in_specs=[
            whole((3, 512, 512)),
            pl.BlockSpec((3, 8, 64, 512), lambda s: (0, s, 0, 0)),
        ],
        out_specs=pl.BlockSpec((128, 8, 256), lambda s: (0, 0, s)),
        out_shape=jax.ShapeDtypeStruct((128, 8, 1024), BF16),
        scratch_shapes=[pltpu.VMEM((2, 16, 32, 256), F32)],
        compiler_params=params(58 * 1024 * 1024),
        name="cubes",
    )(r_pairs, w)


def owner_bits(h, c_h):
    row = lax.broadcasted_iota(jnp.int32, (8, 128), 0)
    value = (2 * row + c_h) ^ h
    return [((value >> t) & 1) == 1 for t in range(4)]


def owner_kernel(
    energy_ref, ec_ref, m_ref, perm_ref, turn_ref, out_ref,
    mf_ref, mp_ref, part_ref, table_ref, eb_ref, s_ref, turned_ref, q_ref, comb_ref,
):
    h, g = lax.axis_index("ba"), lax.axis_index("col")
    lane = lax.broadcasted_iota(jnp.int32, (8, 128), 1)
    lanes = lane_bits(g)
    rows = [owner_bits(h, c_h) for c_h in range(2)]
    shift = energy_ref[512]

    @pl.loop(0, 4)
    def _(part):
        columns = pl.ds(pl.multiple_of(256 * part, 256), 256)
        moved = jnp.dot(
            m_ref[...].reshape(1024, 1024), perm_ref[:, columns], preferred_element_type=F32
        )
        for odd in range(2):
            x = 2 * part + odd
            for j in range(8):
                for i in range(16):
                    row = 8 * (8 * i + j)
                    mp_ref[x, pl.ds(129 * (row // 128) + row % 128, 8), :] = moved[
                        row : row + 8, 128 * odd : 128 * odd + 128
                    ]
                    column = pl.ds(pl.multiple_of(256 * part + 128 * odd, 128), 128)
                    mf_ref[x, i, 9 * j : 9 * j + 8, :] = m_ref[8 * i + j, :, column].astype(F32)
        for a_r in range(4):
            for odd in range(2):
                x = 2 * part + odd
                values = [
                    jnp.full((8, 128), shift - energy_ref[32 * i + 4 * x + a_r], F32)
                    for i in range(16)
                ]
                for i, value in enumerate(butterfly(values, rows[0])):
                    part_ref[x, i, a_r] = value
        for odd in range(2):
            x = 2 * part + odd
            for i in range(16):
                b = [jnp.full((1, 128), energy_ref[32 * i + 4 * x + r], F32) for r in range(4)]
                low = jnp.where(lane[0:1] < 32, b[0], b[1])
                high = jnp.where(lane[0:1] < 96, b[2], b[3])
                eb_ref[x, i : i + 1] = jnp.where(lane[0:1] < 64, low, high)

    @pl.loop(0, 8)
    def _(pair):
        for odd in range(2):
            i = 2 * pair + odd
            for a_r in range(4):
                sums = []
                for c_h in range(2):
                    sums.append([
                        mf_ref[x, i, pl.ds(4 * c_h + a_r, 8, stride=9), :]
                        + mp_ref[x, pl.ds(64 * c_h + 4 * i + a_r, 8, stride=129), :]
                        for x in range(8)
                    ])
                crossed = [butterfly(values, lanes) for values in sums]
                for x in range(8):
                    s_ref[x, i, a_r] = jnp.concatenate([sums[0][x], sums[1][x]], axis=0).astype(BF16)
                    turned_ref[x, i, :, 128 * a_r : 128 * a_r + 128] = jnp.concatenate(
                        [crossed[0][x], crossed[1][x]], axis=0
                    ).astype(BF16)
                values = butterfly([part_ref[x, i, a_r] for x in range(8)], lanes)
                for x in range(8):
                    table_ref[x, i, a_r] = values[x]

    for half in range(2):
        q_ref[...] = jnp.dot(
            turned_ref[...].reshape(2048, 512),
            turn_ref[:, 256 * half : 256 * half + 256],
            preferred_element_type=F32,
        ).reshape(8, 16, 16, 256)

        @pl.loop(0, 8)
        def _(x, half=half):
            for odd in range(2):
                a_r = 2 * half + odd
                for c_h in range(2):
                    values = [
                        q_ref[x, i, 8 * c_h : 8 * c_h + 8, 128 * odd : 128 * odd + 128]
                        for i in range(16)
                    ]
                    values = butterfly(values, rows[c_h])
                    for i in range(16):
                        total = s_ref[x, i, a_r, 8 * c_h : 8 * c_h + 8, :].astype(F32) + values[i]
                        den = (table_ref[x, i ^ c_h, a_r] - eb_ref[x, i : i + 1]) - ec_ref[c_h]
                        comb_ref[x, i, pl.ds(9 * (4 * c_h + a_r), 8), :] = total / den

    @pl.loop(0, 16)
    def _(i):
        for j in range(8):
            for x in range(8):
                value = comb_ref[x, i, pl.ds(j, 8, stride=9), :]
                out_ref[8 * i + j, :, 128 * x : 128 * x + 128] = value.astype(BF16)


VMEM_SPEC = pl.BlockSpec(memory_space=pltpu.VMEM)


def combine_at_owner(energy, ec, m):
    source = np.arange(1024)
    perm = ((source % 32) * 32 + source // 32)[:, None] == source[None, :]
    source = np.arange(512)
    turned = (source // 32 % 4) * 128 + (source // 128) * 32 + source % 32
    turn = turned[:, None] == source[None, :]
    return pl.pallas_call(
        owner_kernel,
        in_specs=[SMEM_SPEC, VMEM_SPEC, VMEM_SPEC, VMEM_SPEC, VMEM_SPEC],
        out_specs=VMEM_SPEC,
        out_shape=jax.ShapeDtypeStruct((128, 8, 1024), BF16),
        scratch_shapes=[
            pltpu.VMEM((8, 16, 72, 128), F32),
            pltpu.VMEM((8, 1032, 128), F32),
            pltpu.VMEM((8, 16, 4, 8, 128), F32),
            pltpu.VMEM((8, 16, 4, 8, 128), F32),
            pltpu.VMEM((8, 16, 128), F32),
            pltpu.VMEM((8, 16, 4, 16, 128), BF16),
            pltpu.VMEM((8, 16, 16, 512), BF16),
            pltpu.VMEM((8, 16, 16, 256), F32),
            pltpu.VMEM((8, 16, 72, 128), F32),
        ],
        compiler_params=params(40 * 1024 * 1024),
        name="combine_at_owner",
    )(energy, ec, m, jnp.asarray(perm, BF16), jnp.asarray(turn, BF16))


def contract_kernel(m_ref, w_ref, out_ref, comb_ref, sum_ref):
    step = pl.program_id(0)
    base = lax.axis_index("ba") ^ (2 * lax.axis_index("col"))
    top = lax.broadcasted_iota(jnp.int32, (8, 128), 0) < 4
    masks = lane_bits(0)

    @pl.loop(0, 16)
    def _(a_hi):
        h = a_hi ^ base
        for tile in range(2):
            lanes = slice(128 * tile, 128 * tile + 128)
            values = []
            for k in range(8):
                g = k ^ (2 * step + tile)
                values.append(m_ref[8 * h + g, :, lanes].astype(F32))
            values = butterfly(values, masks)
            for t in range(2):
                first = halves(values[4 * t], values[4 * t + 1], top)
                second = halves(values[4 * t + 2], values[4 * t + 3], top)
                for half in range(2):
                    rows = jnp.concatenate([first[half], second[half]], axis=0).astype(BF16)
                    comb_ref[half, a_hi ^ half, 16 * t : 16 * t + 16, lanes] = rows

    for m in range(3):
        term = None
        for half in range(2):
            rows = w_ref[m, :, 32 * half : 32 * half + 32, :].reshape(256, 512)
            left = comb_ref[half].reshape(512, 256)
            product = jnp.dot(left, rows, preferred_element_type=F32)
            term = product if term is None else term + product

        @pl.when(step == 0)
        def _(m=m, term=term):
            sum_ref[m] = term

        @pl.when(step > 0)
        def _(m=m, term=term):
            sum_ref[m] = sum_ref[m] + term

    @pl.when(step == 3)
    def _():
        low = lax.broadcasted_iota(jnp.int32, (16, 128), 1) < 64
        for m in range(3):
            for k in range(16):
                for t in range(4):
                    column = slice(128 * t, 128 * t + 128)
                    upper = sum_ref[m, 32 * k : 32 * k + 16, column]
                    lower = sum_ref[m, 32 * k + 16 : 32 * k + 32, column]
                    even = jnp.where(low, upper, pltpu.roll(lower, 64, 1))
                    odd = jnp.where(low, pltpu.roll(upper, 64, 1), lower)
                    out_ref[k, 2 * t, 16 * m : 16 * m + 16, :] = even.astype(BF16)
                    out_ref[k, 2 * t + 1, 16 * m : 16 * m + 16, :] = odd.astype(BF16)


def contract(m, w):
    return pl.pallas_call(
        contract_kernel,
        grid=(4,),
        in_specs=[
            pl.BlockSpec((128, 8, 256), lambda s: (0, 0, s)),
            pl.BlockSpec((3, 8, 64, 512), lambda s: (0, s, 0, 0)),
        ],
        out_specs=whole((16, 8, 48, 128)),
        out_shape=jax.ShapeDtypeStruct((16, 8, 48, 128), BF16),
        scratch_shapes=[pltpu.VMEM((2, 16, 32, 256), BF16), pltpu.VMEM((3, 512, 512), F32)],
        compiler_params=params(),
        name="contract",
    )(m, w)


def total_kernel(parts_ref, out_ref):
    total = parts_ref[0:8].astype(F32).sum(axis=0)
    for s in range(1, 16):
        total = total + parts_ref[8 * s : 8 * s + 8].astype(F32).sum(axis=0)
    for m in range(3):
        out_ref[m, 0:16, :] = total[16 * m : 16 * m + 16, 0:64]
        out_ref[m, 16:32, :] = total[16 * m : 16 * m + 16, 64:128]


def total_of(parts):
    return pl.pallas_call(
        total_kernel,
        out_shape=jax.ShapeDtypeStruct((3, 32, 64), F32),
        compiler_params=pltpu.CompilerParams(vmem_limit_bytes=VMEM_LIMIT),
        name="total",
    )(parts)


def exchange(x, axis):
    return lax.all_to_all(x, axis, split_axis=0, concat_axis=0, tiled=True)


def on_device(r_pairs, w_tiles, virt_energy, energy_shift):
    w = w_tiles[0]
    ec = jnp.broadcast_to(virt_energy.reshape(8, 2, 1, 32), (8, 2, 4, 32))
    ec = jnp.swapaxes(ec.reshape(8, 2, 128), 0, 1)
    energy = jnp.concatenate([virt_energy, jnp.broadcast_to(energy_shift, (128,))])
    cubes, ec, energy = lax.optimization_barrier((make_cubes(r_pairs[0], w), ec, energy))
    met = exchange(cubes, ("ba", "col"))
    combined = combine_at_owner(energy, ec, met)
    home = exchange(combined, ("ba", "col"))
    arrived = exchange(contract(home, w).reshape(128, 48, 128), ("ba", "col"))
    return total_of(arrived)[None]


def solution(mesh):
    in_specs = (P(), P(None, None, "ba", "col", None), P(), P())
    out_specs = P(None, None, "ba", "col")
    return jax.shard_map(
        on_device, mesh=mesh, in_specs=in_specs, out_specs=out_specs, check_vma=False
    )
```

```python
import jax
import jax.numpy as jnp
import numpy as np
from jax import lax
from jax.experimental import pallas as pl
from jax.experimental.pallas import tpu as pltpu
from jax.sharding import Mesh
from jax.sharding import PartitionSpec as P

F32 = jnp.float32
BF16 = jnp.bfloat16
VMEM_LIMIT = 24 * 1024 * 1024


BA = ("xl", "y", "core")
COL = ("xh", "z")


def place():
    i = (lax.axis_index("xl") * 4 + lax.axis_index("y")) * 2 + lax.axis_index("core")
    return i, lax.axis_index("xh") * 4 + lax.axis_index("z")


def lane_bits(g):
    lane = lax.broadcasted_iota(jnp.int32, (8, 128), 1)
    value = ((lane >> 2) & 7) ^ g
    return [((value >> t) & 1) == 1 for t in range(3)]


def butterfly(values, masks):
    for t, mask in enumerate(masks):
        bit = 1 << t
        values = [jnp.where(mask, values[k ^ bit], values[k]) for k in range(len(values))]
    return values


def halves(first, second, top):
    return (
        jnp.where(top, first, pltpu.roll(second, 4, 0)),
        jnp.where(top, pltpu.roll(first, 4, 0), second),
    )


def group_select(lane, bit, low, high):
    keep = (lane & bit) == 0
    first = jnp.where(keep, low, pltpu.roll(high, bit, 1))
    second = jnp.where(keep, pltpu.roll(low, 128 - bit, 1), high)
    return first, second


def whole(shape):
    return pl.BlockSpec(shape, lambda s: (0,) * len(shape), pipeline_mode=pl.Buffered(1))


def params(limit=VMEM_LIMIT):
    return pltpu.CompilerParams(vmem_limit_bytes=limit)


SMEM_SPEC = pl.BlockSpec(memory_space=pltpu.SMEM)


def cube_kernel(r_ref, w_ref, out_ref, x_ref):
    step = pl.program_id(0)
    i, j = place()
    base = i ^ (2 * j)
    top = lax.broadcasted_iota(jnp.int32, (8, 128), 0) < 4
    masks = lane_bits(0)

    def multiply():
        for half in range(2):
            acc = None
            for m in range(3):
                rows = w_ref[m, :, 32 * half : 32 * half + 32, :].reshape(256, 512)
                term = lax.dot_general(
                    r_ref[m], rows, (((1,), (1,)), ((), ())), preferred_element_type=F32
                )
                acc = term if acc is None else acc + term
            x_ref[step % 2, half] = acc.reshape(16, 32, 256)

    def send():
        old = (step + 1) % 2
        for a_hi in range(16):
            h = a_hi ^ base
            for tile in range(2):
                lanes = slice(128 * tile, 128 * tile + 128)
                values = []
                for t in range(4):
                    values += halves(
                        x_ref[old, 0, a_hi, 8 * t : 8 * t + 8, lanes],
                        x_ref[old, 1, a_hi ^ 1, 8 * t : 8 * t + 8, lanes],
                        top,
                    )
                for k, value in enumerate(butterfly(values, masks)):
                    g = k ^ (2 * (step - 1) + tile)
                    out_ref[8 * h + g, :, lanes] = value.astype(BF16)

    in_turn(step, multiply, send)


def in_turn(step, first, second):
    @pl.when(step == 0)
    def _():
        first()

    @pl.when((step > 0) & (step < 4))
    def _():
        second()
        first()

    @pl.when(step == 4)
    def _():
        second()


def make_cubes(r_pairs, w):
    return pl.pallas_call(
        cube_kernel,
        grid=(5,),
        in_specs=[
            whole((3, 512, 512)),
            pl.BlockSpec((3, 8, 64, 512), lambda s: (0, jnp.minimum(s, 3), 0, 0)),
        ],
        out_specs=pl.BlockSpec((128, 8, 256), lambda s: (0, 0, jnp.maximum(s - 1, 0))),
        out_shape=jax.ShapeDtypeStruct((128, 8, 1024), BF16),
        scratch_shapes=[pltpu.VMEM((2, 2, 16, 32, 256), F32)],
        compiler_params=params(58 * 1024 * 1024),
        cost_estimate=pl.CostEstimate(
            flops=2 * 512 * 2048 * 1536, bytes_accessed=10 * 1024**2, transcendentals=0
        ),
        name="cubes",
    )(r_pairs, w)


def owner_bits(h, c_h):
    row = lax.broadcasted_iota(jnp.int32, (8, 128), 0)
    value = (2 * row + c_h) ^ h
    return [((value >> t) & 1) == 1 for t in range(4)]


def owner_kernel(
    energy_ref, ec_ref, m_ref, perm_ref, turn_ref, out_ref,
    mf_ref, mp_ref, part_ref, table_ref, eb_ref, s_ref, turned_ref, q_ref, comb_ref,
):
    h, g = place()
    lane = lax.broadcasted_iota(jnp.int32, (8, 128), 1)
    lanes = lane_bits(g)
    rows = [owner_bits(h, c_h) for c_h in range(2)]
    shift = energy_ref[512]

    @pl.loop(0, 4)
    def _(part):
        columns = pl.ds(pl.multiple_of(256 * part, 256), 256)
        moved = jnp.dot(
            m_ref[...].reshape(1024, 1024), perm_ref[:, columns], preferred_element_type=F32
        )
        for odd in range(2):
            x = 2 * part + odd
            for j in range(8):
                for i in range(16):
                    row = 8 * (8 * i + j)
                    mp_ref[x, pl.ds(129 * (row // 128) + row % 128, 8), :] = moved[
                        row : row + 8, 128 * odd : 128 * odd + 128
                    ]
                    column = pl.ds(pl.multiple_of(256 * part + 128 * odd, 128), 128)
                    mf_ref[x, i, 9 * j : 9 * j + 8, :] = m_ref[8 * i + j, :, column].astype(F32)
        for a_r in range(4):
            for odd in range(2):
                x = 2 * part + odd
                values = [
                    jnp.full((8, 128), shift - energy_ref[32 * i + 4 * x + a_r], F32)
                    for i in range(16)
                ]
                for i, value in enumerate(butterfly(values, rows[0])):
                    part_ref[x, i, a_r] = value
        for odd in range(2):
            x = 2 * part + odd
            for i in range(16):
                b = [jnp.full((1, 128), energy_ref[32 * i + 4 * x + r], F32) for r in range(4)]
                low = jnp.where(lane[0:1] < 32, b[0], b[1])
                high = jnp.where(lane[0:1] < 96, b[2], b[3])
                eb_ref[x, i : i + 1] = jnp.where(lane[0:1] < 64, low, high)

    @pl.loop(0, 8)
    def _(pair):
        for odd in range(2):
            i = 2 * pair + odd
            for a_r in range(4):
                sums = []
                for c_h in range(2):
                    sums.append([
                        mf_ref[x, i, pl.ds(4 * c_h + a_r, 8, stride=9), :]
                        + mp_ref[x, pl.ds(64 * c_h + 4 * i + a_r, 8, stride=129), :]
                        for x in range(8)
                    ])
                crossed = [butterfly(values, lanes) for values in sums]
                for x in range(8):
                    s_ref[x, i, a_r] = jnp.concatenate([sums[0][x], sums[1][x]], axis=0).astype(BF16)
                    turned_ref[x, i, :, 128 * a_r : 128 * a_r + 128] = jnp.concatenate(
                        [crossed[0][x], crossed[1][x]], axis=0
                    ).astype(BF16)
                values = butterfly([part_ref[x, i, a_r] for x in range(8)], lanes)
                for x in range(8):
                    table_ref[x, i, a_r] = values[x]

    for half in range(2):
        q_ref[...] = jnp.dot(
            turned_ref[...].reshape(2048, 512),
            turn_ref[:, 256 * half : 256 * half + 256],
            preferred_element_type=F32,
        ).reshape(8, 16, 16, 256)

        @pl.loop(0, 8)
        def _(x, half=half):
            for odd in range(2):
                a_r = 2 * half + odd
                for c_h in range(2):
                    values = [
                        q_ref[x, i, 8 * c_h : 8 * c_h + 8, 128 * odd : 128 * odd + 128]
                        for i in range(16)
                    ]
                    values = butterfly(values, rows[c_h])
                    for i in range(16):
                        total = s_ref[x, i, a_r, 8 * c_h : 8 * c_h + 8, :].astype(F32) + values[i]
                        den = (table_ref[x, i ^ c_h, a_r] - eb_ref[x, i : i + 1]) - ec_ref[c_h]
                        comb_ref[x, i ^ c_h ^ (h & 1), pl.ds(9 * (4 * c_h + a_r), 8), :] = total / den

    @pl.loop(0, 16)
    def _(i):
        for j in range(8):
            for x in range(8):
                value = comb_ref[x, i, pl.ds(j, 8, stride=9), :]
                out_ref[8 * i + j, :, 128 * x : 128 * x + 128] = value.astype(BF16)


VMEM_SPEC = pl.BlockSpec(memory_space=pltpu.VMEM)


def combine_at_owner(energy, ec, m):
    source = np.arange(1024)
    perm = ((source % 32) * 32 + source // 32)[:, None] == source[None, :]
    source = np.arange(512)
    turned = (source // 32 % 4) * 128 + (source // 128) * 32 + source % 32
    turn = turned[:, None] == source[None, :]
    return pl.pallas_call(
        owner_kernel,
        in_specs=[SMEM_SPEC, VMEM_SPEC, VMEM_SPEC, VMEM_SPEC, VMEM_SPEC],
        out_specs=VMEM_SPEC,
        out_shape=jax.ShapeDtypeStruct((128, 8, 1024), BF16),
        scratch_shapes=[
            pltpu.VMEM((8, 16, 72, 128), F32),
            pltpu.VMEM((8, 1032, 128), F32),
            pltpu.VMEM((8, 16, 4, 8, 128), F32),
            pltpu.VMEM((8, 16, 4, 8, 128), F32),
            pltpu.VMEM((8, 16, 128), F32),
            pltpu.VMEM((8, 16, 4, 16, 128), BF16),
            pltpu.VMEM((8, 16, 16, 512), BF16),
            pltpu.VMEM((8, 16, 16, 256), F32),
            pltpu.VMEM((8, 16, 72, 128), F32),
        ],
        compiler_params=params(40 * 1024 * 1024),
        name="combine_at_owner",
    )(energy, ec, m, jnp.asarray(perm, BF16), jnp.asarray(turn, BF16))


def contract_kernel(m_ref, w_ref, other_ref, out_ref, comb_ref, sum_ref):
    step = pl.program_id(0)
    i, j = place()
    base = (i >> 1) ^ j
    top = lax.broadcasted_iota(jnp.int32, (8, 128), 0) < 4
    masks = lane_bits(0)

    def receive():
        for block in range(8):
            for low in range(2):
                h = 2 * (block ^ base) + low
                for tile in range(2):
                    lanes = slice(128 * tile, 128 * tile + 128)
                    values = []
                    for k in range(8):
                        g = k ^ (2 * step + tile)
                        values.append(m_ref[8 * h + g, :, lanes].astype(F32))
                    values = butterfly(values, masks)
                    for t in range(2):
                        first = halves(values[4 * t], values[4 * t + 1], top)
                        second = halves(values[4 * t + 2], values[4 * t + 3], top)
                        for half in range(2):
                            start = 512 * (low ^ half) + 256 * half + 128 * tile
                            rows = jnp.concatenate([first[half], second[half]], axis=0)
                            row = 32 * block + 16 * t
                            comb_ref[step % 2, row : row + 16, start : start + 128] = rows.astype(BF16)

    def multiply():
        for m in range(3):
            rows = [
                ref[m, :, 32 * half : 32 * half + 32, :].reshape(256, 512)
                for ref in (w_ref, other_ref)
                for half in range(2)
            ]
            term = jnp.dot(
                comb_ref[(step + 1) % 2], jnp.concatenate(rows, axis=0), preferred_element_type=F32
            )
            sum_ref[m] = term + jnp.where(step > 1, sum_ref[m], 0.0)

    in_turn(step, receive, multiply)

    @pl.when(step == 4)
    def _():
        low = lax.broadcasted_iota(jnp.int32, (16, 128), 1) < 64
        for m in range(3):
            for k in range(8):
                for t in range(4):
                    column = slice(128 * t, 128 * t + 128)
                    upper = sum_ref[m, 32 * k : 32 * k + 16, column]
                    lower = sum_ref[m, 32 * k + 16 : 32 * k + 32, column]
                    even = jnp.where(low, upper, pltpu.roll(lower, 64, 1))
                    odd = jnp.where(low, pltpu.roll(upper, 64, 1), lower)
                    out_ref[k, 2 * t, 16 * m : 16 * m + 16, :] = even.astype(BF16)
                    out_ref[k, 2 * t + 1, 16 * m : 16 * m + 16, :] = odd.astype(BF16)


def contract(m, w, other):
    behind = pl.BlockSpec((3, 8, 64, 512), lambda s: (0, jnp.maximum(s - 1, 0), 0, 0))
    return pl.pallas_call(
        contract_kernel,
        grid=(5,),
        in_specs=[
            pl.BlockSpec((128, 8, 256), lambda s: (0, 0, jnp.minimum(s, 3))),
            behind,
            behind,
        ],
        out_specs=whole((8, 8, 48, 128)),
        out_shape=jax.ShapeDtypeStruct((8, 8, 48, 128), BF16),
        scratch_shapes=[pltpu.VMEM((2, 256, 1024), BF16), pltpu.VMEM((3, 256, 512), F32)],
        compiler_params=params(),
        name="contract",
    )(m, w, other)


def total_kernel(parts_ref, out_ref):
    total = parts_ref[0:8].astype(F32).sum(axis=0)
    for s in range(1, 8):
        total = total + parts_ref[8 * s : 8 * s + 8].astype(F32).sum(axis=0)
    for m in range(3):
        out_ref[m, 0:16, :] = total[16 * m : 16 * m + 16, 0:64]
        out_ref[m, 16:32, :] = total[16 * m : 16 * m + 16, 64:128]


def total_of(parts):
    return pl.pallas_call(
        total_kernel,
        out_shape=jax.ShapeDtypeStruct((3, 32, 64), F32),
        compiler_params=pltpu.CompilerParams(vmem_limit_bytes=VMEM_LIMIT),
        name="total",
    )(parts)


def exchange(x, axis):
    return lax.all_to_all(x, axis, split_axis=0, concat_axis=0, tiled=True)


def on_device(r_pairs, w_tiles, virt_energy, energy_shift):
    w = w_tiles[0]
    other = lax.ppermute(w, "core", [(0, 1), (1, 0)])
    ec = jnp.broadcast_to(virt_energy.reshape(8, 2, 1, 32), (8, 2, 4, 32))
    ec = jnp.swapaxes(ec.reshape(8, 2, 128), 0, 1)
    energy = jnp.concatenate([virt_energy, jnp.broadcast_to(energy_shift, (128,))])
    cubes, ec, energy = lax.optimization_barrier((make_cubes(r_pairs[0], w), ec, energy))
    met = exchange(cubes, BA + COL)
    home = exchange(combine_at_owner(energy, ec, met), BA + COL)
    parts = contract(home, w, other).reshape(64, 48, 128)
    return total_of(exchange(parts, ("xl", "y") + COL))[None]


def solution(mesh):
    mesh = Mesh(mesh.devices.reshape(2, 4, 2, 2, 4), BA + COL)
    in_specs = (P(), P(None, None, BA, COL, None), P(), P())
    out_specs = P(None, None, BA, COL)
    return jax.shard_map(
        on_device, mesh=mesh, in_specs=in_specs, out_specs=out_specs, check_vma=False
    )
```

```python
import jax
import jax.numpy as jnp
import numpy as np
from jax import lax
from jax.experimental import pallas as pl
from jax.experimental.pallas import tpu as pltpu
from jax.sharding import Mesh
from jax.sharding import PartitionSpec as P

F32 = jnp.float32
BF16 = jnp.bfloat16
VMEM_LIMIT = 24 * 1024 * 1024


BA = ("xl", "y", "core")
COL = ("xh", "z")


def place():
    i = (lax.axis_index("xl") * 4 + lax.axis_index("y")) * 2 + lax.axis_index("core")
    return i, lax.axis_index("xh") * 4 + lax.axis_index("z")


def lane_bits(g):
    lane = lax.broadcasted_iota(jnp.int32, (8, 128), 1)
    value = ((lane >> 2) & 7) ^ g
    return [((value >> t) & 1) == 1 for t in range(3)]


def butterfly(values, masks):
    for t, mask in enumerate(masks):
        bit = 1 << t
        values = [jnp.where(mask, values[k ^ bit], values[k]) for k in range(len(values))]
    return values


def halves(first, second, top):
    return (
        jnp.where(top, first, pltpu.roll(second, 4, 0)),
        jnp.where(top, pltpu.roll(first, 4, 0), second),
    )


def group_select(lane, bit, low, high):
    keep = (lane & bit) == 0
    first = jnp.where(keep, low, pltpu.roll(high, bit, 1))
    second = jnp.where(keep, pltpu.roll(low, 128 - bit, 1), high)
    return first, second


def whole(shape):
    return pl.BlockSpec(shape, lambda s: (0,) * len(shape), pipeline_mode=pl.Buffered(1))


def params(limit=VMEM_LIMIT):
    return pltpu.CompilerParams(vmem_limit_bytes=limit)


SMEM_SPEC = pl.BlockSpec(memory_space=pltpu.SMEM)


def cube_kernel(r_ref, w_ref, _, out_ref, x_ref):
    step = pl.program_id(0)
    i, j = place()
    base = i ^ (2 * j)
    top = lax.broadcasted_iota(jnp.int32, (8, 128), 0) < 4
    masks = lane_bits(0)

    def multiply():
        for half in range(2):
            acc = None
            for m in range(3):
                rows = w_ref[m, :, 32 * half : 32 * half + 32, :].reshape(256, 512)
                term = lax.dot_general(
                    r_ref[m], rows, (((1,), (1,)), ((), ())), preferred_element_type=F32
                )
                acc = term if acc is None else acc + term
            x_ref[step % 2, half] = acc.reshape(16, 32, 256)

    def send():
        old = (step + 1) % 2
        for a_hi in range(16):
            h = a_hi ^ base
            for tile in range(2):
                lanes = slice(128 * tile, 128 * tile + 128)
                values = []
                for t in range(4):
                    values += halves(
                        x_ref[old, 0, a_hi, 8 * t : 8 * t + 8, lanes],
                        x_ref[old, 1, a_hi ^ 1, 8 * t : 8 * t + 8, lanes],
                        top,
                    )
                for k, value in enumerate(butterfly(values, masks)):
                    g = k ^ (2 * (step - 1) + tile)
                    out_ref[8 * h + g, :, lanes] = value.astype(BF16)

    in_turn(step, multiply, send)


def in_turn(step, first, second):
    @pl.when(step == 0)
    def _():
        first()

    @pl.when((step > 0) & (step < 4))
    def _():
        second()
        first()

    @pl.when(step == 4)
    def _():
        second()


def make_cubes(r_pairs, w, shift):
    return pl.pallas_call(
        cube_kernel,
        grid=(5,),
        in_specs=[
            whole((3, 512, 512)),
            pl.BlockSpec((3, 8, 64, 512), lambda s: (0, jnp.minimum(s, 3), 0, 0)),
            whole((1, 1)),
        ],
        out_specs=pl.BlockSpec((128, 8, 256), lambda s: (0, 0, jnp.maximum(s - 1, 0))),
        out_shape=jax.ShapeDtypeStruct((128, 8, 1024), BF16),
        scratch_shapes=[pltpu.VMEM((2, 2, 16, 32, 256), F32)],
        compiler_params=params(58 * 1024 * 1024),
        cost_estimate=pl.CostEstimate(
            flops=2 * 512 * 2048 * 1536, bytes_accessed=10 * 1024**2, transcendentals=0
        ),
        name="cubes",
    )(r_pairs, w, shift)


def owner_bits(h, c_h):
    row = lax.broadcasted_iota(jnp.int32, (8, 128), 0)
    value = (2 * row + c_h) ^ h
    return [((value >> t) & 1) == 1 for t in range(4)]


def owner_kernel(
    energy_ref, rows_ref, shift_ref, m_ref, perm_ref, turn_ref, out_ref,
    ec_ref, mf_ref, mp_ref, part_ref, table_ref, eb_ref, s_ref, turned_ref, q0_ref, q1_ref, comb_ref,
):
    h, g = place()
    lane = lax.broadcasted_iota(jnp.int32, (8, 128), 1)
    lanes = lane_bits(g)
    rows = [owner_bits(h, c_h) for c_h in range(2)]
    shift = jnp.broadcast_to(shift_ref[...], (8, 128))

    twice = jnp.concatenate([rows_ref[...], rows_ref[...]], axis=0)
    for source in range(4):
        spread = twice
        for step in range(1, 4):
            there = lane // 32 == (source + step) % 4
            spread = jnp.where(there, pltpu.roll(twice, 32 * step, 1), spread)
        for row in range(4):
            j = 2 * row + source // 2
            ec_ref[source % 2, j : j + 1] = spread[row : row + 1]

    @pl.loop(0, 2)
    def _(part):
        columns = pl.ds(pl.multiple_of(512 * part, 512), 512)
        moved = jnp.dot(
            m_ref[...].reshape(1024, 1024), perm_ref[:, columns], preferred_element_type=F32
        )
        for tile in range(4):
            x = 4 * part + tile
            for j in range(8):
                for i in range(16):
                    row = 8 * (8 * i + j)
                    mp_ref[x, pl.ds(129 * (row // 128) + row % 128, 8), :] = moved[
                        row : row + 8, 128 * tile : 128 * tile + 128
                    ]
                    column = pl.ds(pl.multiple_of(512 * part + 128 * tile, 128), 128)
                    mf_ref[x, i, 9 * j : 9 * j + 8, :] = m_ref[8 * i + j, :, column].astype(F32)
        for a_r in range(4):
            for tile in range(4):
                x = 4 * part + tile
                values = [
                    shift - energy_ref[i // 4, 32 * (i % 4) + 4 * x + a_r]
                    for i in range(16)
                ]
                for i, value in enumerate(butterfly(values, rows[0])):
                    part_ref[x, i, a_r] = value
        for tile in range(4):
            x = 4 * part + tile
            for i in range(16):
                b = [jnp.full((1, 128), energy_ref[i // 4, 32 * (i % 4) + 4 * x + r], F32) for r in range(4)]
                low = jnp.where(lane[0:1] < 32, b[0], b[1])
                high = jnp.where(lane[0:1] < 96, b[2], b[3])
                eb_ref[x, i : i + 1] = jnp.where(lane[0:1] < 64, low, high)

    @pl.loop(0, 8)
    def _(pair):
        for odd in range(2):
            i = 2 * pair + odd
            for a_r in range(4):
                sums = []
                for c_h in range(2):
                    sums.append([
                        mf_ref[x, i, pl.ds(4 * c_h + a_r, 8, stride=9), :]
                        + mp_ref[x, pl.ds(64 * c_h + 4 * i + a_r, 8, stride=129), :]
                        for x in range(8)
                    ])
                crossed = [butterfly(values, lanes) for values in sums]
                for x in range(8):
                    s_ref[x, i, a_r] = jnp.concatenate([sums[0][x], sums[1][x]], axis=0).astype(BF16)
                    turned_ref[x, i, :, 128 * a_r : 128 * a_r + 128] = jnp.concatenate(
                        [crossed[0][x], crossed[1][x]], axis=0
                    ).astype(BF16)
                values = butterfly([part_ref[x, i, a_r] for x in range(8)], lanes)
                for x in range(8):
                    table_ref[x, i, a_r] = values[x]

    def turn(x, q_ref):
        q_ref[...] = jnp.dot(
            turned_ref[x].reshape(256, 512), turn_ref[...], preferred_element_type=F32
        ).reshape(16, 16, 512)

    def divide(x, q_ref):
        for a_r in range(4):
            for c_h in range(2):
                values = [
                    q_ref[i, 8 * c_h : 8 * c_h + 8, 128 * a_r : 128 * a_r + 128] for i in range(16)
                ]
                values = butterfly(values, rows[c_h])
                for i in range(16):
                    total = s_ref[x, i, a_r, 8 * c_h : 8 * c_h + 8, :].astype(F32) + values[i]
                    den = (table_ref[x, i ^ c_h, a_r] - eb_ref[x, i : i + 1]) - ec_ref[c_h]
                    comb_ref[x, i ^ c_h ^ (h & 1), pl.ds(9 * (4 * c_h + a_r), 8), :] = total / den

    turn(0, q0_ref)

    @pl.loop(0, 4)
    def _(pair):
        turn(2 * pair + 1, q1_ref)
        divide(2 * pair, q0_ref)
        turn(jnp.minimum(2 * pair + 2, 7), q0_ref)
        divide(2 * pair + 1, q1_ref)

    @pl.loop(0, 16)
    def _(i):
        for j in range(8):
            for x in range(8):
                value = comb_ref[x, i, pl.ds(j, 8, stride=9), :]
                out_ref[8 * i + j, :, 128 * x : 128 * x + 128] = value.astype(BF16)


VMEM_SPEC = pl.BlockSpec(memory_space=pltpu.VMEM)


def combine_at_owner(energy, shift, m):
    source = np.arange(1024)
    perm = ((source % 32) * 32 + source // 32)[:, None] == source[None, :]
    source = np.arange(512)
    turned = (source // 32 % 4) * 128 + (source // 128) * 32 + source % 32
    turn = turned[:, None] == source[None, :]
    return pl.pallas_call(
        owner_kernel,
        in_specs=[SMEM_SPEC] + [VMEM_SPEC] * 5,
        out_specs=VMEM_SPEC,
        out_shape=jax.ShapeDtypeStruct((128, 8, 1024), BF16),
        scratch_shapes=[
            pltpu.VMEM((2, 8, 128), F32),
            pltpu.VMEM((8, 16, 72, 128), F32),
            pltpu.VMEM((8, 1032, 128), F32),
            pltpu.VMEM((8, 16, 4, 8, 128), F32),
            pltpu.VMEM((8, 16, 4, 8, 128), F32),
            pltpu.VMEM((8, 16, 128), F32),
            pltpu.VMEM((8, 16, 4, 16, 128), BF16),
            pltpu.VMEM((8, 16, 16, 512), BF16),
            pltpu.VMEM((16, 16, 512), F32),
            pltpu.VMEM((16, 16, 512), F32),
            pltpu.VMEM((8, 16, 72, 128), F32),
        ],
        compiler_params=params(40 * 1024 * 1024),
        name="combine_at_owner",
    )(energy, energy, shift, m, jnp.asarray(perm, BF16), jnp.asarray(turn, BF16))


def contract_kernel(m_ref, w_ref, other_ref, out_ref, comb_ref, sum_ref):
    step = pl.program_id(0)
    i, j = place()
    base = (i >> 1) ^ j
    top = lax.broadcasted_iota(jnp.int32, (8, 128), 0) < 4
    masks = lane_bits(0)

    def receive():
        for block in range(8):
            for low in range(2):
                h = 2 * (block ^ base) + low
                for tile in range(2):
                    lanes = slice(128 * tile, 128 * tile + 128)
                    values = []
                    for k in range(8):
                        g = k ^ (2 * step + tile)
                        values.append(m_ref[8 * h + g, :, lanes].astype(F32))
                    values = butterfly(values, masks)
                    for t in range(2):
                        first = halves(values[4 * t], values[4 * t + 1], top)
                        second = halves(values[4 * t + 2], values[4 * t + 3], top)
                        for half in range(2):
                            start = 512 * (low ^ half) + 256 * half + 128 * tile
                            rows = jnp.concatenate([first[half], second[half]], axis=0)
                            row = 32 * block + 16 * t
                            comb_ref[step % 2, row : row + 16, start : start + 128] = rows.astype(BF16)

    def multiply():
        for m in range(3):
            rows = [
                ref[m, :, 32 * half : 32 * half + 32, :].reshape(256, 512)
                for ref in (w_ref, other_ref)
                for half in range(2)
            ]
            term = jnp.dot(
                comb_ref[(step + 1) % 2], jnp.concatenate(rows, axis=0), preferred_element_type=F32
            )
            sum_ref[m] = term + jnp.where(step > 1, sum_ref[m], 0.0)

    in_turn(step, receive, multiply)

    @pl.when(step == 4)
    def _():
        low = lax.broadcasted_iota(jnp.int32, (16, 128), 1) < 64
        for m in range(3):
            for k in range(8):
                for t in range(4):
                    column = slice(128 * t, 128 * t + 128)
                    upper = sum_ref[m, 32 * k : 32 * k + 16, column]
                    lower = sum_ref[m, 32 * k + 16 : 32 * k + 32, column]
                    even = jnp.where(low, upper, pltpu.roll(lower, 64, 1))
                    odd = jnp.where(low, pltpu.roll(upper, 64, 1), lower)
                    out_ref[k, 2 * t, 16 * m : 16 * m + 16, :] = even.astype(BF16)
                    out_ref[k, 2 * t + 1, 16 * m : 16 * m + 16, :] = odd.astype(BF16)


def contract(m, w, other):
    behind = pl.BlockSpec((3, 8, 64, 512), lambda s: (0, jnp.maximum(s - 1, 0), 0, 0))
    return pl.pallas_call(
        contract_kernel,
        grid=(5,),
        in_specs=[
            pl.BlockSpec((128, 8, 256), lambda s: (0, 0, jnp.minimum(s, 3))),
            behind,
            behind,
        ],
        out_specs=whole((8, 8, 48, 128)),
        out_shape=jax.ShapeDtypeStruct((8, 8, 48, 128), BF16),
        scratch_shapes=[pltpu.VMEM((2, 256, 1024), BF16), pltpu.VMEM((3, 256, 512), F32)],
        compiler_params=params(),
        name="contract",
    )(m, w, other)


def total_kernel(parts_ref, out_ref):
    total = parts_ref[0:8].astype(F32).sum(axis=0)
    for s in range(1, 8):
        total = total + parts_ref[8 * s : 8 * s + 8].astype(F32).sum(axis=0)
    for m in range(3):
        out_ref[m, 0:16, :] = total[16 * m : 16 * m + 16, 0:64]
        out_ref[m, 16:32, :] = total[16 * m : 16 * m + 16, 64:128]


def total_of(parts):
    return pl.pallas_call(
        total_kernel,
        out_shape=jax.ShapeDtypeStruct((3, 32, 64), F32),
        compiler_params=pltpu.CompilerParams(vmem_limit_bytes=VMEM_LIMIT),
        name="total",
    )(parts)


def exchange(x, axis):
    return lax.all_to_all(x, axis, split_axis=0, concat_axis=0, tiled=True)


def on_device(r_pairs, w_tiles, virt_energy, energy_shift):
    w = w_tiles[0]
    energy, shift = virt_energy.reshape(4, 128), energy_shift.reshape(1, 1)
    cubes, later = lax.optimization_barrier((make_cubes(r_pairs[0], w, shift), w))
    other = lax.ppermute(later, "core", [(0, 1), (1, 0)])
    met = exchange(cubes, BA + COL)
    home = exchange(combine_at_owner(energy, shift, met), BA + COL)
    parts = contract(home, w, other).reshape(64, 48, 128)
    return total_of(exchange(parts, ("xl", "y") + COL))[None]


def solution(mesh):
    mesh = Mesh(mesh.devices.reshape(2, 4, 2, 2, 4), BA + COL)
    in_specs = (P(), P(None, None, BA, COL, None), P(), P())
    out_specs = P(None, None, BA, COL)
    return jax.shard_map(
        on_device, mesh=mesh, in_specs=in_specs, out_specs=out_specs, check_vma=False
    )
```

```python
import jax
import jax.numpy as jnp
import numpy as np
from jax import lax
from jax.experimental import pallas as pl
from jax.experimental.pallas import tpu as pltpu
from jax.sharding import Mesh
from jax.sharding import PartitionSpec as P

F32 = jnp.float32
BF16 = jnp.bfloat16
VMEM_LIMIT = 24 * 1024 * 1024


BA = ("xl", "y", "core")
COL = ("xh", "z")


def place():
    i = (lax.axis_index("xl") * 4 + lax.axis_index("y")) * 2 + lax.axis_index("core")
    return i, lax.axis_index("xh") * 4 + lax.axis_index("z")


def lane_bits(g):
    lane = lax.broadcasted_iota(jnp.int32, (8, 128), 1)
    value = ((lane >> 2) & 7) ^ g
    return [((value >> t) & 1) == 1 for t in range(3)]


def butterfly(values, masks):
    for t, mask in enumerate(masks):
        bit = 1 << t
        values = [jnp.where(mask, values[k ^ bit], values[k]) for k in range(len(values))]
    return values


def halves(first, second, top):
    return (
        jnp.where(top, first, pltpu.roll(second, 4, 0)),
        jnp.where(top, pltpu.roll(first, 4, 0), second),
    )


def group_select(lane, bit, low, high):
    keep = (lane & bit) == 0
    first = jnp.where(keep, low, pltpu.roll(high, bit, 1))
    second = jnp.where(keep, pltpu.roll(low, 128 - bit, 1), high)
    return first, second


def whole(shape):
    return pl.BlockSpec(shape, lambda s: (0,) * len(shape), pipeline_mode=pl.Buffered(1))


def params(limit=VMEM_LIMIT):
    return pltpu.CompilerParams(vmem_limit_bytes=limit)


SMEM_SPEC = pl.BlockSpec(memory_space=pltpu.SMEM)


def cube_kernel(r_ref, w_ref, _, out_ref, x_ref):
    step = pl.program_id(0)
    i, j = place()
    base = i ^ (2 * j)
    top = lax.broadcasted_iota(jnp.int32, (8, 128), 0) < 4
    masks = lane_bits(0)

    def multiply():
        for half in range(2):
            acc = None
            for m in range(3):
                rows = w_ref[m, :, 32 * half : 32 * half + 32, :].reshape(256, 512)
                term = lax.dot_general(
                    r_ref[m], rows, (((1,), (1,)), ((), ())), preferred_element_type=F32
                )
                acc = term if acc is None else acc + term
            x_ref[step % 2, half] = acc.reshape(16, 32, 256)

    def send():
        old = (step + 1) % 2
        for a_hi in range(16):
            h = a_hi ^ base
            for tile in range(2):
                lanes = slice(128 * tile, 128 * tile + 128)
                values = []
                for t in range(4):
                    values += halves(
                        x_ref[old, 0, a_hi, 8 * t : 8 * t + 8, lanes],
                        x_ref[old, 1, a_hi ^ 1, 8 * t : 8 * t + 8, lanes],
                        top,
                    )
                for k, value in enumerate(butterfly(values, masks)):
                    g = k ^ (2 * (step - 1) + tile)
                    out_ref[8 * h + g, :, lanes] = value.astype(BF16)

    in_turn(step, multiply, send)


def in_turn(step, first, second):
    @pl.when(step == 0)
    def _():
        first()

    @pl.when((step > 0) & (step < 4))
    def _():
        second()
        first()

    @pl.when(step == 4)
    def _():
        second()


def make_cubes(r_pairs, w, shift):
    return pl.pallas_call(
        cube_kernel,
        grid=(5,),
        in_specs=[
            whole((3, 512, 512)),
            pl.BlockSpec((3, 8, 64, 512), lambda s: (0, jnp.minimum(s, 3), 0, 0)),
            whole((1, 1)),
        ],
        out_specs=pl.BlockSpec((128, 8, 256), lambda s: (0, 0, jnp.maximum(s - 1, 0))),
        out_shape=jax.ShapeDtypeStruct((128, 8, 1024), BF16),
        scratch_shapes=[pltpu.VMEM((2, 2, 16, 32, 256), F32)],
        compiler_params=params(58 * 1024 * 1024),
        cost_estimate=pl.CostEstimate(
            flops=2 * 512 * 2048 * 1536, bytes_accessed=10 * 1024**2, transcendentals=0
        ),
        name="cubes",
    )(r_pairs, w, shift)


def owner_bits(h, c_h):
    row = lax.broadcasted_iota(jnp.int32, (8, 128), 0)
    value = (2 * row + c_h) ^ h
    return [((value >> t) & 1) == 1 for t in range(4)]


def owner_kernel(
    energy_ref, rows_ref, shift_ref, m_ref, perm_ref, turn_ref, out_ref,
    ec_ref, mf_ref, mp_ref, part_ref, table_ref, eb_ref, s_ref, turned_ref, q0_ref, q1_ref, comb_ref,
):
    h, g = place()
    lane = lax.broadcasted_iota(jnp.int32, (8, 128), 1)
    lanes = lane_bits(g)
    rows = [owner_bits(h, c_h) for c_h in range(2)]
    shift = jnp.broadcast_to(shift_ref[...], (8, 128))

    twice = jnp.concatenate([rows_ref[...], rows_ref[...]], axis=0)
    for source in range(4):
        spread = twice
        for step in range(1, 4):
            there = lane // 32 == (source + step) % 4
            spread = jnp.where(there, pltpu.roll(twice, 32 * step, 1), spread)
        for row in range(4):
            j = 2 * row + source // 2
            ec_ref[source % 2, j : j + 1] = spread[row : row + 1]

    @pl.loop(0, 2)
    def _(part):
        columns = pl.ds(pl.multiple_of(512 * part, 512), 512)
        moved = jnp.dot(
            m_ref[...].reshape(1024, 1024), perm_ref[:, columns], preferred_element_type=F32
        )
        for tile in range(4):
            x = 4 * part + tile
            for j in range(8):
                for i in range(16):
                    row = 8 * (8 * i + j)
                    mp_ref[x, pl.ds(129 * (row // 128) + row % 128, 8), :] = moved[
                        row : row + 8, 128 * tile : 128 * tile + 128
                    ]
                    column = pl.ds(pl.multiple_of(512 * part + 128 * tile, 128), 128)
                    mf_ref[x, i, 9 * j : 9 * j + 8, :] = m_ref[8 * i + j, :, column].astype(F32)
        for a_r in range(4):
            for tile in range(4):
                x = 4 * part + tile
                values = [
                    shift - energy_ref[i // 4, 32 * (i % 4) + 4 * x + a_r]
                    for i in range(16)
                ]
                for i, value in enumerate(butterfly(values, rows[0])):
                    part_ref[x, i, a_r] = value
        for tile in range(4):
            x = 4 * part + tile
            for i in range(16):
                b = [jnp.full((1, 128), energy_ref[i // 4, 32 * (i % 4) + 4 * x + r], F32) for r in range(4)]
                low = jnp.where(lane[0:1] < 32, b[0], b[1])
                high = jnp.where(lane[0:1] < 96, b[2], b[3])
                eb_ref[x, i : i + 1] = jnp.where(lane[0:1] < 64, low, high)

    @pl.loop(0, 8)
    def _(pair):
        for odd in range(2):
            i = 2 * pair + odd
            for a_r in range(4):
                sums = []
                for c_h in range(2):
                    sums.append([
                        mf_ref[x, i, pl.ds(4 * c_h + a_r, 8, stride=9), :]
                        + mp_ref[x, pl.ds(64 * c_h + 4 * i + a_r, 8, stride=129), :]
                        for x in range(8)
                    ])
                crossed = [butterfly(values, lanes) for values in sums]
                for x in range(8):
                    s_ref[x, i, a_r] = jnp.concatenate([sums[0][x], sums[1][x]], axis=0).astype(BF16)
                    turned_ref[x, i, :, 128 * a_r : 128 * a_r + 128] = jnp.concatenate(
                        [crossed[0][x], crossed[1][x]], axis=0
                    ).astype(BF16)
                values = butterfly([part_ref[x, i, a_r] for x in range(8)], lanes)
                for x in range(8):
                    table_ref[x, i, a_r] = values[x]

    def turn(x, q_ref):
        q_ref[...] = jnp.dot(
            turned_ref[x].reshape(256, 512), turn_ref[...], preferred_element_type=F32
        ).reshape(16, 16, 512)

    def divide(x, q_ref):
        for a_r in range(4):
            for c_h in range(2):
                values = [
                    q_ref[i, 8 * c_h : 8 * c_h + 8, 128 * a_r : 128 * a_r + 128] for i in range(16)
                ]
                values = butterfly(values, rows[c_h])
                for i in range(16):
                    total = s_ref[x, i, a_r, 8 * c_h : 8 * c_h + 8, :].astype(F32) + values[i]
                    den = (table_ref[x, i ^ c_h, a_r] - eb_ref[x, i : i + 1]) - ec_ref[c_h]
                    comb_ref[x, i ^ c_h ^ (h & 1), pl.ds(9 * (4 * c_h + a_r), 8), :] = total / den

    turn(0, q0_ref)

    @pl.loop(0, 4)
    def _(pair):
        turn(2 * pair + 1, q1_ref)
        divide(2 * pair, q0_ref)
        turn(jnp.minimum(2 * pair + 2, 7), q0_ref)
        divide(2 * pair + 1, q1_ref)

    @pl.loop(0, 16)
    def _(i):
        for j in range(8):
            for x in range(8):
                value = comb_ref[x, i, pl.ds(j, 8, stride=9), :]
                out_ref[8 * i + j, :, 128 * x : 128 * x + 128] = value.astype(BF16)


VMEM_SPEC = pl.BlockSpec(memory_space=pltpu.VMEM)


def combine_at_owner(energy, shift, m):
    source = np.arange(1024)
    perm = ((source % 32) * 32 + source // 32)[:, None] == source[None, :]
    source = np.arange(512)
    turned = (source // 32 % 4) * 128 + (source // 128) * 32 + source % 32
    turn = turned[:, None] == source[None, :]
    return pl.pallas_call(
        owner_kernel,
        in_specs=[SMEM_SPEC] + [VMEM_SPEC] * 5,
        out_specs=VMEM_SPEC,
        out_shape=jax.ShapeDtypeStruct((128, 8, 1024), BF16),
        scratch_shapes=[
            pltpu.VMEM((2, 8, 128), F32),
            pltpu.VMEM((8, 16, 80, 128), F32),
            pltpu.VMEM((8, 1160, 128), F32),
            pltpu.VMEM((8, 16, 4, 8, 128), F32),
            pltpu.VMEM((8, 16, 4, 8, 128), F32),
            pltpu.VMEM((8, 16, 128), F32),
            pltpu.VMEM((8, 16, 4, 16, 128), BF16),
            pltpu.VMEM((8, 16, 16, 512), BF16),
            pltpu.VMEM((16, 16, 512), F32),
            pltpu.VMEM((16, 16, 512), F32),
            pltpu.VMEM((8, 16, 80, 128), F32),
        ],
        compiler_params=params(40 * 1024 * 1024),
        name="combine_at_owner",
    )(energy, energy, shift, m, jnp.asarray(perm, BF16), jnp.asarray(turn, BF16))


def contract_kernel(m_ref, w_ref, other_ref, out_ref, comb_ref, sum_ref):
    step = pl.program_id(0)
    i, j = place()
    base = (i >> 1) ^ j
    top = lax.broadcasted_iota(jnp.int32, (8, 128), 0) < 4
    masks = lane_bits(0)

    def receive():
        for block in range(8):
            for low in range(2):
                h = 2 * (block ^ base) + low
                for tile in range(2):
                    lanes = slice(128 * tile, 128 * tile + 128)
                    values = []
                    for k in range(8):
                        g = k ^ (2 * step + tile)
                        values.append(m_ref[8 * h + g, :, lanes].astype(F32))
                    values = butterfly(values, masks)
                    for t in range(2):
                        first = halves(values[4 * t], values[4 * t + 1], top)
                        second = halves(values[4 * t + 2], values[4 * t + 3], top)
                        for half in range(2):
                            start = 512 * (low ^ half) + 256 * half + 128 * tile
                            rows = jnp.concatenate([first[half], second[half]], axis=0)
                            row = 32 * block + 16 * t
                            comb_ref[step % 2, row : row + 16, start : start + 128] = rows.astype(BF16)

    def multiply():
        for m in range(3):
            rows = [
                ref[m, :, 32 * half : 32 * half + 32, :].reshape(256, 512)
                for ref in (w_ref, other_ref)
                for half in range(2)
            ]
            term = jnp.dot(
                comb_ref[(step + 1) % 2], jnp.concatenate(rows, axis=0), preferred_element_type=F32
            )
            sum_ref[m] = term + jnp.where(step > 1, sum_ref[m], 0.0)

    in_turn(step, receive, multiply)

    @pl.when(step == 4)
    def _():
        low = lax.broadcasted_iota(jnp.int32, (16, 128), 1) < 64
        for m in range(3):
            for k in range(8):
                for t in range(4):
                    column = slice(128 * t, 128 * t + 128)
                    upper = sum_ref[m, 32 * k : 32 * k + 16, column]
                    lower = sum_ref[m, 32 * k + 16 : 32 * k + 32, column]
                    even = jnp.where(low, upper, pltpu.roll(lower, 64, 1))
                    odd = jnp.where(low, pltpu.roll(upper, 64, 1), lower)
                    out_ref[k, 2 * t, 16 * m : 16 * m + 16, :] = even.astype(BF16)
                    out_ref[k, 2 * t + 1, 16 * m : 16 * m + 16, :] = odd.astype(BF16)


def contract(m, w, other):
    behind = pl.BlockSpec((3, 8, 64, 512), lambda s: (0, jnp.maximum(s - 1, 0), 0, 0))
    return pl.pallas_call(
        contract_kernel,
        grid=(5,),
        in_specs=[
            pl.BlockSpec((128, 8, 256), lambda s: (0, 0, jnp.minimum(s, 3))),
            behind,
            behind,
        ],
        out_specs=whole((8, 8, 48, 128)),
        out_shape=jax.ShapeDtypeStruct((8, 8, 48, 128), BF16),
        scratch_shapes=[pltpu.VMEM((2, 256, 1024), BF16), pltpu.VMEM((3, 256, 512), F32)],
        compiler_params=params(),
        name="contract",
    )(m, w, other)


def total_kernel(parts_ref, out_ref):
    total = parts_ref[0:8].astype(F32).sum(axis=0)
    for s in range(1, 8):
        total = total + parts_ref[8 * s : 8 * s + 8].astype(F32).sum(axis=0)
    for m in range(3):
        out_ref[m, 0:16, :] = total[16 * m : 16 * m + 16, 0:64]
        out_ref[m, 16:32, :] = total[16 * m : 16 * m + 16, 64:128]


def total_of(parts):
    return pl.pallas_call(
        total_kernel,
        out_shape=jax.ShapeDtypeStruct((3, 32, 64), F32),
        compiler_params=pltpu.CompilerParams(vmem_limit_bytes=VMEM_LIMIT),
        name="total",
    )(parts)


def exchange(x, axis):
    return lax.all_to_all(x, axis, split_axis=0, concat_axis=0, tiled=True)


def on_device(r_pairs, w_tiles, virt_energy, energy_shift):
    w = w_tiles[0]
    energy, shift = virt_energy.reshape(4, 128), energy_shift.reshape(1, 1)
    cubes, later = lax.optimization_barrier((make_cubes(r_pairs[0], w, shift), w))
    other = lax.ppermute(later, "core", [(0, 1), (1, 0)])
    met = exchange(cubes, BA + COL)
    home = exchange(combine_at_owner(energy, shift, met), BA + COL)
    parts = contract(home, w, other).reshape(64, 48, 128)
    return total_of(exchange(parts, ("xl", "y") + COL))[None]


def solution(mesh):
    mesh = Mesh(mesh.devices.reshape(2, 4, 2, 2, 4), BA + COL)
    in_specs = (P(), P(None, None, BA, COL, None), P(), P())
    out_specs = P(None, None, BA, COL)
    return jax.shard_map(
        on_device, mesh=mesh, in_specs=in_specs, out_specs=out_specs, check_vma=False
    )
```

```python
import jax
import jax.numpy as jnp
import numpy as np
from jax import lax
from jax.experimental import pallas as pl
from jax.experimental.pallas import tpu as pltpu
from jax.sharding import Mesh
from jax.sharding import PartitionSpec as P

F32 = jnp.float32
BF16 = jnp.bfloat16
VMEM_LIMIT = 24 * 1024 * 1024


BA = ("xl", "y", "core")
COL = ("xh", "z")


def place():
    i = (lax.axis_index("xl") * 4 + lax.axis_index("y")) * 2 + lax.axis_index("core")
    return i, lax.axis_index("xh") * 4 + lax.axis_index("z")


def lane_bits(g):
    lane = lax.broadcasted_iota(jnp.int32, (8, 128), 1)
    value = ((lane >> 2) & 7) ^ g
    return [((value >> t) & 1) == 1 for t in range(3)]


def butterfly(values, masks):
    for t, mask in enumerate(masks):
        bit = 1 << t
        values = [jnp.where(mask, values[k ^ bit], values[k]) for k in range(len(values))]
    return values


def halves(first, second, top):
    return (
        jnp.where(top, first, pltpu.roll(second, 4, 0)),
        jnp.where(top, pltpu.roll(first, 4, 0), second),
    )


def group_select(lane, bit, low, high):
    keep = (lane & bit) == 0
    first = jnp.where(keep, low, pltpu.roll(high, bit, 1))
    second = jnp.where(keep, pltpu.roll(low, 128 - bit, 1), high)
    return first, second


def whole(shape):
    return pl.BlockSpec(shape, lambda s: (0,) * len(shape), pipeline_mode=pl.Buffered(1))


def params(limit=VMEM_LIMIT):
    return pltpu.CompilerParams(vmem_limit_bytes=limit)


SMEM_SPEC = pl.BlockSpec(memory_space=pltpu.SMEM)


def cube_kernel(r_ref, w_ref, _, out_ref, x_ref):
    step = pl.program_id(0)
    i, j = place()
    base = i ^ (2 * j)
    top = lax.broadcasted_iota(jnp.int32, (8, 128), 0) < 4
    masks = lane_bits(0)

    def multiply():
        for half in range(2):
            acc = None
            for m in range(3):
                rows = w_ref[m, :, 32 * half : 32 * half + 32, :].reshape(256, 512)
                term = lax.dot_general(
                    r_ref[m], rows, (((1,), (1,)), ((), ())), preferred_element_type=F32
                )
                acc = term if acc is None else acc + term
            x_ref[step % 2, half] = acc.reshape(16, 32, 256)

    def send():
        old = (step + 1) % 2
        for a_hi in range(16):
            h = a_hi ^ base
            for tile in range(2):
                lanes = slice(128 * tile, 128 * tile + 128)
                values = []
                for t in range(4):
                    values += halves(
                        x_ref[old, 0, a_hi, 8 * t : 8 * t + 8, lanes],
                        x_ref[old, 1, a_hi ^ 1, 8 * t : 8 * t + 8, lanes],
                        top,
                    )
                for k, value in enumerate(butterfly(values, masks)):
                    g = k ^ (2 * (step - 1) + tile)
                    out_ref[8 * h + g, :, lanes] = value.astype(BF16)

    in_turn(step, multiply, send)


def in_turn(step, first, second):
    @pl.when(step == 0)
    def _():
        first()

    @pl.when((step > 0) & (step < 4))
    def _():
        second()
        first()

    @pl.when(step == 4)
    def _():
        second()


def make_cubes(r_pairs, w, shift):
    return pl.pallas_call(
        cube_kernel,
        grid=(5,),
        in_specs=[
            whole((3, 512, 512)),
            pl.BlockSpec((3, 8, 64, 512), lambda s: (0, jnp.minimum(s, 3), 0, 0)),
            whole((1, 1)),
        ],
        out_specs=pl.BlockSpec((128, 8, 256), lambda s: (0, 0, jnp.maximum(s - 1, 0))),
        out_shape=jax.ShapeDtypeStruct((128, 8, 1024), BF16),
        scratch_shapes=[pltpu.VMEM((2, 2, 16, 32, 256), F32)],
        compiler_params=params(58 * 1024 * 1024),
        cost_estimate=pl.CostEstimate(
            flops=2 * 512 * 2048 * 1536, bytes_accessed=10 * 1024**2, transcendentals=0
        ),
        name="cubes",
    )(r_pairs, w, shift)


def owner_bits(h, c_h):
    row = lax.broadcasted_iota(jnp.int32, (8, 128), 0)
    value = (2 * row + c_h) ^ h
    return [((value >> t) & 1) == 1 for t in range(4)]


def owner_kernel(
    energy_ref, rows_ref, shift_ref, m_ref, perm_ref, turn_ref, out_ref,
    ec_ref, mf_ref, mp_ref, part_ref, table_ref, eb_ref, s_ref, turned_ref, q0_ref, q1_ref, comb_ref,
):
    h, g = place()
    lane = lax.broadcasted_iota(jnp.int32, (8, 128), 1)
    lanes = lane_bits(g)
    rows = [owner_bits(h, c_h) for c_h in range(2)]
    shift = jnp.broadcast_to(shift_ref[...], (8, 128))

    twice = jnp.concatenate([rows_ref[...], rows_ref[...]], axis=0)
    for source in range(4):
        spread = twice
        for step in range(1, 4):
            there = lane // 32 == (source + step) % 4
            spread = jnp.where(there, pltpu.roll(twice, 32 * step, 1), spread)
        for row in range(4):
            j = 2 * row + source // 2
            ec_ref[source % 2, j : j + 1] = spread[row : row + 1]

    @pl.loop(0, 2)
    def _(part):
        columns = pl.ds(pl.multiple_of(512 * part, 512), 512)
        moved = jnp.dot(
            m_ref[...].reshape(1024, 1024), perm_ref[:, columns], preferred_element_type=F32
        )
        for tile in range(4):
            x = 4 * part + tile
            for j in range(8):
                for i in range(16):
                    row = 8 * (8 * i + j)
                    mp_ref[x, pl.ds(129 * (row // 128) + row % 128, 8), :] = moved[
                        row : row + 8, 128 * tile : 128 * tile + 128
                    ]
        for a_r in range(4):
            for tile in range(4):
                x = 4 * part + tile
                values = [
                    shift - energy_ref[i // 4, 32 * (i % 4) + 4 * x + a_r]
                    for i in range(16)
                ]
                for i, value in enumerate(butterfly(values, rows[0])):
                    part_ref[x, i, a_r] = value
        for tile in range(4):
            x = 4 * part + tile
            for i in range(16):
                b = [jnp.full((1, 128), energy_ref[i // 4, 32 * (i % 4) + 4 * x + r], F32) for r in range(4)]
                low = jnp.where(lane[0:1] < 32, b[0], b[1])
                high = jnp.where(lane[0:1] < 96, b[2], b[3])
                eb_ref[x, i : i + 1] = jnp.where(lane[0:1] < 64, low, high)

    @pl.loop(0, 16)
    def _(i):
        for j in range(8):
            for x in range(8):
                block = m_ref[8 * i + j, :, 128 * x : 128 * x + 128]
                mf_ref[x, i, 9 * j : 9 * j + 8, :] = block.astype(F32)

    @pl.loop(0, 8)
    def _(pair):
        for odd in range(2):
            i = 2 * pair + odd
            for a_r in range(4):
                sums = []
                for c_h in range(2):
                    sums.append([
                        mf_ref[x, i, pl.ds(4 * c_h + a_r, 8, stride=9), :]
                        + mp_ref[x, pl.ds(64 * c_h + 4 * i + a_r, 8, stride=129), :]
                        for x in range(8)
                    ])
                crossed = [butterfly(values, lanes) for values in sums]
                for x in range(8):
                    s_ref[x, i, a_r] = jnp.concatenate([sums[0][x], sums[1][x]], axis=0).astype(BF16)
                    turned_ref[x, i, :, 128 * a_r : 128 * a_r + 128] = jnp.concatenate(
                        [crossed[0][x], crossed[1][x]], axis=0
                    ).astype(BF16)
                values = butterfly([part_ref[x, i, a_r] for x in range(8)], lanes)
                for x in range(8):
                    table_ref[x, i, a_r] = values[x]

    def turn(x, q_ref):
        q_ref[...] = jnp.dot(
            turned_ref[x].reshape(256, 512), turn_ref[...], preferred_element_type=F32
        ).reshape(16, 16, 512)

    def divide(x, q_ref):
        for a_r in range(4):
            for c_h in range(2):
                values = [
                    q_ref[i, 8 * c_h : 8 * c_h + 8, 128 * a_r : 128 * a_r + 128] for i in range(16)
                ]
                values = butterfly(values, rows[c_h])
                for i in range(16):
                    total = s_ref[x, i, a_r, 8 * c_h : 8 * c_h + 8, :].astype(F32) + values[i]
                    den = (table_ref[x, i ^ c_h, a_r] - eb_ref[x, i : i + 1]) - ec_ref[c_h]
                    comb_ref[x, i ^ c_h ^ (h & 1), pl.ds(9 * (4 * c_h + a_r), 8), :] = total / den

    turn(0, q0_ref)

    @pl.loop(0, 4)
    def _(pair):
        turn(2 * pair + 1, q1_ref)
        divide(2 * pair, q0_ref)
        turn(jnp.minimum(2 * pair + 2, 7), q0_ref)
        divide(2 * pair + 1, q1_ref)

    @pl.loop(0, 16)
    def _(i):
        for j in range(8):
            for x in range(8):
                value = comb_ref[x, i, pl.ds(j, 8, stride=9), :]
                out_ref[8 * i + j, :, 128 * x : 128 * x + 128] = value.astype(BF16)


VMEM_SPEC = pl.BlockSpec(memory_space=pltpu.VMEM)


def combine_at_owner(energy, shift, m):
    source = np.arange(1024)
    perm = ((source % 32) * 32 + source // 32)[:, None] == source[None, :]
    source = np.arange(512)
    turned = (source // 32 % 4) * 128 + (source // 128) * 32 + source % 32
    turn = turned[:, None] == source[None, :]
    return pl.pallas_call(
        owner_kernel,
        in_specs=[SMEM_SPEC] + [VMEM_SPEC] * 5,
        out_specs=VMEM_SPEC,
        out_shape=jax.ShapeDtypeStruct((128, 8, 1024), BF16),
        scratch_shapes=[
            pltpu.VMEM((2, 8, 128), F32),
            pltpu.VMEM((8, 16, 80, 128), F32),
            pltpu.VMEM((8, 1160, 128), F32),
            pltpu.VMEM((8, 16, 4, 8, 128), F32),
            pltpu.VMEM((8, 16, 4, 8, 128), F32),
            pltpu.VMEM((8, 16, 128), F32),
            pltpu.VMEM((8, 16, 4, 16, 128), BF16),
            pltpu.VMEM((8, 16, 16, 512), BF16),
            pltpu.VMEM((16, 16, 512), F32),
            pltpu.VMEM((16, 16, 512), F32),
            pltpu.VMEM((8, 16, 80, 128), F32),
        ],
        compiler_params=params(40 * 1024 * 1024),
        name="combine_at_owner",
    )(energy, energy, shift, m, jnp.asarray(perm, BF16), jnp.asarray(turn, BF16))


def contract_kernel(m_ref, w_ref, other_ref, out_ref, comb_ref, sum_ref):
    step = pl.program_id(0)
    i, j = place()
    base = (i >> 1) ^ j
    top = lax.broadcasted_iota(jnp.int32, (8, 128), 0) < 4
    masks = lane_bits(0)

    def receive():
        for block in range(8):
            for low in range(2):
                h = 2 * (block ^ base) + low
                for tile in range(2):
                    lanes = slice(128 * tile, 128 * tile + 128)
                    values = []
                    for k in range(8):
                        g = k ^ (2 * step + tile)
                        values.append(m_ref[8 * h + g, :, lanes].astype(F32))
                    values = butterfly(values, masks)
                    for t in range(2):
                        first = halves(values[4 * t], values[4 * t + 1], top)
                        second = halves(values[4 * t + 2], values[4 * t + 3], top)
                        for half in range(2):
                            start = 512 * (low ^ half) + 256 * half + 128 * tile
                            rows = jnp.concatenate([first[half], second[half]], axis=0)
                            row = 32 * block + 16 * t
                            comb_ref[step % 2, row : row + 16, start : start + 128] = rows.astype(BF16)

    def multiply():
        for m in range(3):
            rows = [
                ref[m, :, 32 * half : 32 * half + 32, :].reshape(256, 512)
                for ref in (w_ref, other_ref)
                for half in range(2)
            ]
            term = jnp.dot(
                comb_ref[(step + 1) % 2], jnp.concatenate(rows, axis=0), preferred_element_type=F32
            )
            sum_ref[m] = term + jnp.where(step > 1, sum_ref[m], 0.0)

    in_turn(step, receive, multiply)

    @pl.when(step == 4)
    def _():
        low = lax.broadcasted_iota(jnp.int32, (16, 128), 1) < 64
        for m in range(3):
            for k in range(8):
                for t in range(4):
                    column = slice(128 * t, 128 * t + 128)
                    upper = sum_ref[m, 32 * k : 32 * k + 16, column]
                    lower = sum_ref[m, 32 * k + 16 : 32 * k + 32, column]
                    even = jnp.where(low, upper, pltpu.roll(lower, 64, 1))
                    odd = jnp.where(low, pltpu.roll(upper, 64, 1), lower)
                    out_ref[k, 2 * t, 16 * m : 16 * m + 16, :] = even.astype(BF16)
                    out_ref[k, 2 * t + 1, 16 * m : 16 * m + 16, :] = odd.astype(BF16)


def contract(m, w, other):
    behind = pl.BlockSpec((3, 8, 64, 512), lambda s: (0, jnp.maximum(s - 1, 0), 0, 0))
    return pl.pallas_call(
        contract_kernel,
        grid=(5,),
        in_specs=[
            pl.BlockSpec((128, 8, 256), lambda s: (0, 0, jnp.minimum(s, 3))),
            behind,
            behind,
        ],
        out_specs=whole((8, 8, 48, 128)),
        out_shape=jax.ShapeDtypeStruct((8, 8, 48, 128), BF16),
        scratch_shapes=[pltpu.VMEM((2, 256, 1024), BF16), pltpu.VMEM((3, 256, 512), F32)],
        compiler_params=params(),
        name="contract",
    )(m, w, other)


def total_kernel(parts_ref, out_ref):
    total = parts_ref[0:8].astype(F32).sum(axis=0)
    for s in range(1, 8):
        total = total + parts_ref[8 * s : 8 * s + 8].astype(F32).sum(axis=0)
    for m in range(3):
        out_ref[m, 0:16, :] = total[16 * m : 16 * m + 16, 0:64]
        out_ref[m, 16:32, :] = total[16 * m : 16 * m + 16, 64:128]


def total_of(parts):
    return pl.pallas_call(
        total_kernel,
        out_shape=jax.ShapeDtypeStruct((3, 32, 64), F32),
        compiler_params=pltpu.CompilerParams(vmem_limit_bytes=VMEM_LIMIT),
        name="total",
    )(parts)


def exchange(x, axis):
    return lax.all_to_all(x, axis, split_axis=0, concat_axis=0, tiled=True)


def on_device(r_pairs, w_tiles, virt_energy, energy_shift):
    w = w_tiles[0]
    energy, shift = virt_energy.reshape(4, 128), energy_shift.reshape(1, 1)
    cubes, later = lax.optimization_barrier((make_cubes(r_pairs[0], w, shift), w))
    other = lax.ppermute(later, "core", [(0, 1), (1, 0)])
    met = exchange(cubes, BA + COL)
    home = exchange(combine_at_owner(energy, shift, met), BA + COL)
    parts = contract(home, w, other).reshape(64, 48, 128)
    return total_of(exchange(parts, ("xl", "y") + COL))[None]


def solution(mesh):
    mesh = Mesh(mesh.devices.reshape(2, 4, 2, 2, 4), BA + COL)
    in_specs = (P(), P(None, None, BA, COL, None), P(), P())
    out_specs = P(None, None, BA, COL)
    return jax.shard_map(
        on_device, mesh=mesh, in_specs=in_specs, out_specs=out_specs, check_vma=False
    )
```

```python
import jax
import jax.numpy as jnp
import numpy as np
from jax import lax
from jax.experimental import pallas as pl
from jax.experimental.pallas import tpu as pltpu
from jax.sharding import Mesh
from jax.sharding import PartitionSpec as P

F32 = jnp.float32
BF16 = jnp.bfloat16
VMEM_LIMIT = 24 * 1024 * 1024


BA = ("xl", "y", "core")
COL = ("xh", "z")


def place():
    i = (lax.axis_index("xl") * 4 + lax.axis_index("y")) * 2 + lax.axis_index("core")
    return i, lax.axis_index("xh") * 4 + lax.axis_index("z")


def lane_bits(g):
    lane = lax.broadcasted_iota(jnp.int32, (8, 128), 1)
    value = ((lane >> 2) & 7) ^ g
    return [((value >> t) & 1) == 1 for t in range(3)]


def butterfly(values, masks):
    for t, mask in enumerate(masks):
        bit = 1 << t
        values = [jnp.where(mask, values[k ^ bit], values[k]) for k in range(len(values))]
    return values


def halves(first, second, top):
    return (
        jnp.where(top, first, pltpu.roll(second, 4, 0)),
        jnp.where(top, pltpu.roll(first, 4, 0), second),
    )


def group_select(lane, bit, low, high):
    keep = (lane & bit) == 0
    first = jnp.where(keep, low, pltpu.roll(high, bit, 1))
    second = jnp.where(keep, pltpu.roll(low, 128 - bit, 1), high)
    return first, second


def whole(shape):
    return pl.BlockSpec(shape, lambda s: (0,) * len(shape), pipeline_mode=pl.Buffered(1))


def params(limit=VMEM_LIMIT):
    return pltpu.CompilerParams(vmem_limit_bytes=limit)


SMEM_SPEC = pl.BlockSpec(memory_space=pltpu.SMEM)


def cube_kernel(r_ref, w_ref, _, out_ref, x_ref):
    step = pl.program_id(0)
    i, j = place()
    base = i ^ (2 * j)
    top = lax.broadcasted_iota(jnp.int32, (8, 128), 0) < 4
    masks = lane_bits(0)

    def multiply():
        for half in range(2):
            acc = None
            for m in range(3):
                rows = w_ref[m, :, 32 * half : 32 * half + 32, :].reshape(512, 512)
                term = lax.dot_general(
                    r_ref[m], rows, (((1,), (1,)), ((), ())), preferred_element_type=F32
                )
                acc = term if acc is None else acc + term
            x_ref[step % 2, half] = acc.reshape(16, 32, 512)

    def send():
        old = (step + 1) % 2
        for a_hi in range(16):
            h = a_hi ^ base
            for tile in range(4):
                lanes = slice(128 * tile, 128 * tile + 128)
                values = []
                for t in range(4):
                    values += halves(
                        x_ref[old, 0, a_hi, 8 * t : 8 * t + 8, lanes],
                        x_ref[old, 1, a_hi ^ 1, 8 * t : 8 * t + 8, lanes],
                        top,
                    )
                for k, value in enumerate(butterfly(values, masks)):
                    g = k ^ (4 * (step - 1) + tile)
                    out_ref[8 * h + g, :, lanes] = value.astype(BF16)

    in_turn(step, 2, multiply, send)


def in_turn(step, count, first, second):
    @pl.when(step == 0)
    def _():
        first()

    @pl.when((step > 0) & (step < count))
    def _():
        second()
        first()

    @pl.when(step == count)
    def _():
        second()


def make_cubes(r_pairs, w, shift):
    return pl.pallas_call(
        cube_kernel,
        grid=(3,),
        in_specs=[
            whole((3, 512, 512)),
            pl.BlockSpec((3, 16, 64, 512), lambda s: (0, jnp.minimum(s, 1), 0, 0)),
            whole((1, 1)),
        ],
        out_specs=pl.BlockSpec((128, 8, 512), lambda s: (0, 0, jnp.maximum(s - 1, 0))),
        out_shape=jax.ShapeDtypeStruct((128, 8, 1024), BF16),
        scratch_shapes=[pltpu.VMEM((2, 2, 16, 32, 512), F32)],
        compiler_params=params(58 * 1024 * 1024),
        cost_estimate=pl.CostEstimate(
            flops=2 * 512 * 2048 * 1536, bytes_accessed=10 * 1024**2, transcendentals=0
        ),
        name="cubes",
    )(r_pairs, w, shift)


def owner_bits(h, c_h):
    row = lax.broadcasted_iota(jnp.int32, (8, 128), 0)
    value = (2 * row + c_h) ^ h
    return [((value >> t) & 1) == 1 for t in range(4)]


def owner_kernel(
    energy_ref, rows_ref, shift_ref, m_ref, perm_ref, turn_ref, out_ref,
    ec_ref, mf_ref, mp_ref, part_ref, table_ref, eb_ref, s_ref, turned_ref, q0_ref, q1_ref, comb_ref,
):
    h, g = place()
    lane = lax.broadcasted_iota(jnp.int32, (8, 128), 1)
    lanes = lane_bits(g)
    rows = [owner_bits(h, c_h) for c_h in range(2)]
    shift = jnp.broadcast_to(shift_ref[...], (8, 128))

    twice = jnp.concatenate([rows_ref[...], rows_ref[...]], axis=0)
    for source in range(4):
        spread = twice
        for step in range(1, 4):
            there = lane // 32 == (source + step) % 4
            spread = jnp.where(there, pltpu.roll(twice, 32 * step, 1), spread)
        for row in range(4):
            j = 2 * row + source // 2
            ec_ref[source % 2, j : j + 1] = spread[row : row + 1]

    @pl.loop(0, 2)
    def _(part):
        columns = pl.ds(pl.multiple_of(512 * part, 512), 512)
        moved = jnp.dot(
            m_ref[...].reshape(1024, 1024), perm_ref[:, columns], preferred_element_type=F32
        )
        for tile in range(4):
            x = 4 * part + tile
            for j in range(8):
                for i in range(16):
                    row = 8 * (8 * i + j)
                    mp_ref[x, pl.ds(129 * (row // 128) + row % 128, 8), :] = moved[
                        row : row + 8, 128 * tile : 128 * tile + 128
                    ]
                    column = pl.ds(pl.multiple_of(512 * part + 128 * tile, 128), 128)
                    mf_ref[x, i, 9 * j : 9 * j + 8, :] = m_ref[8 * i + j, :, column].astype(F32)
        for a_r in range(4):
            for tile in range(4):
                x = 4 * part + tile
                values = [
                    shift - energy_ref[i // 4, 32 * (i % 4) + 4 * x + a_r]
                    for i in range(16)
                ]
                for i, value in enumerate(butterfly(values, rows[0])):
                    part_ref[x, i, a_r] = value
        for tile in range(4):
            x = 4 * part + tile
            for i in range(16):
                b = [jnp.full((1, 128), energy_ref[i // 4, 32 * (i % 4) + 4 * x + r], F32) for r in range(4)]
                low = jnp.where(lane[0:1] < 32, b[0], b[1])
                high = jnp.where(lane[0:1] < 96, b[2], b[3])
                eb_ref[x, i : i + 1] = jnp.where(lane[0:1] < 64, low, high)

    @pl.loop(0, 8)
    def _(pair):
        for odd in range(2):
            i = 2 * pair + odd
            for a_r in range(4):
                sums = []
                for c_h in range(2):
                    sums.append([
                        mf_ref[x, i, pl.ds(4 * c_h + a_r, 8, stride=9), :]
                        + mp_ref[x, pl.ds(64 * c_h + 4 * i + a_r, 8, stride=129), :]
                        for x in range(8)
                    ])
                crossed = [butterfly(values, lanes) for values in sums]
                for x in range(8):
                    s_ref[x, i, a_r] = jnp.concatenate([sums[0][x], sums[1][x]], axis=0).astype(BF16)
                    turned_ref[x, i, :, 128 * a_r : 128 * a_r + 128] = jnp.concatenate(
                        [crossed[0][x], crossed[1][x]], axis=0
                    ).astype(BF16)
                values = butterfly([part_ref[x, i, a_r] for x in range(8)], lanes)
                for x in range(8):
                    table_ref[x, i, a_r] = values[x]

    def turn(x, q_ref):
        q_ref[...] = jnp.dot(
            turned_ref[x].reshape(256, 512), turn_ref[...], preferred_element_type=F32
        ).reshape(16, 16, 512)

    def divide(x, q_ref):
        for a_r in range(4):
            for c_h in range(2):
                values = [
                    q_ref[i, 8 * c_h : 8 * c_h + 8, 128 * a_r : 128 * a_r + 128] for i in range(16)
                ]
                values = butterfly(values, rows[c_h])
                for i in range(16):
                    total = s_ref[x, i, a_r, 8 * c_h : 8 * c_h + 8, :].astype(F32) + values[i]
                    den = (table_ref[x, i ^ c_h, a_r] - eb_ref[x, i : i + 1]) - ec_ref[c_h]
                    comb_ref[x, i ^ c_h ^ (h & 1), pl.ds(9 * (4 * c_h + a_r), 8), :] = total / den

    turn(0, q0_ref)

    @pl.loop(0, 4)
    def _(pair):
        turn(2 * pair + 1, q1_ref)
        divide(2 * pair, q0_ref)
        turn(jnp.minimum(2 * pair + 2, 7), q0_ref)
        divide(2 * pair + 1, q1_ref)

    @pl.loop(0, 16)
    def _(i):
        for j in range(8):
            for x in range(8):
                value = comb_ref[x, i, pl.ds(j, 8, stride=9), :]
                out_ref[8 * i + j, :, 128 * x : 128 * x + 128] = value.astype(BF16)


VMEM_SPEC = pl.BlockSpec(memory_space=pltpu.VMEM)


def combine_at_owner(energy, shift, m):
    source = np.arange(1024)
    perm = ((source % 32) * 32 + source // 32)[:, None] == source[None, :]
    source = np.arange(512)
    turned = (source // 32 % 4) * 128 + (source // 128) * 32 + source % 32
    turn = turned[:, None] == source[None, :]
    return pl.pallas_call(
        owner_kernel,
        in_specs=[SMEM_SPEC] + [VMEM_SPEC] * 5,
        out_specs=VMEM_SPEC,
        out_shape=jax.ShapeDtypeStruct((128, 8, 1024), BF16),
        scratch_shapes=[
            pltpu.VMEM((2, 8, 128), F32),
            pltpu.VMEM((8, 16, 80, 128), F32),
            pltpu.VMEM((8, 1160, 128), F32),
            pltpu.VMEM((8, 16, 4, 8, 128), F32),
            pltpu.VMEM((8, 16, 4, 8, 128), F32),
            pltpu.VMEM((8, 16, 128), F32),
            pltpu.VMEM((8, 16, 4, 16, 128), BF16),
            pltpu.VMEM((8, 16, 16, 512), BF16),
            pltpu.VMEM((16, 16, 512), F32),
            pltpu.VMEM((16, 16, 512), F32),
            pltpu.VMEM((8, 16, 80, 128), F32),
        ],
        compiler_params=params(40 * 1024 * 1024),
        name="combine_at_owner",
    )(energy, energy, shift, m, jnp.asarray(perm, BF16), jnp.asarray(turn, BF16))


def contract_kernel(m_ref, w_ref, other_ref, out_ref, comb_ref, sum_ref):
    step = pl.program_id(0)
    i, j = place()
    base = (i >> 1) ^ j
    top = lax.broadcasted_iota(jnp.int32, (8, 128), 0) < 4
    masks = lane_bits(0)

    def receive():
        for block in range(8):
            for low in range(2):
                h = 2 * (block ^ base) + low
                for tile in range(2):
                    lanes = slice(128 * tile, 128 * tile + 128)
                    values = []
                    for k in range(8):
                        g = k ^ (2 * step + tile)
                        values.append(m_ref[8 * h + g, :, lanes].astype(F32))
                    values = butterfly(values, masks)
                    for t in range(2):
                        first = halves(values[4 * t], values[4 * t + 1], top)
                        second = halves(values[4 * t + 2], values[4 * t + 3], top)
                        for half in range(2):
                            start = 512 * (low ^ half) + 256 * half + 128 * tile
                            rows = jnp.concatenate([first[half], second[half]], axis=0)
                            row = 32 * block + 16 * t
                            comb_ref[step % 2, row : row + 16, start : start + 128] = rows.astype(BF16)

    def multiply():
        for m in range(3):
            rows = [
                ref[m, :, 32 * half : 32 * half + 32, :].reshape(256, 512)
                for ref in (w_ref, other_ref)
                for half in range(2)
            ]
            term = jnp.dot(
                comb_ref[(step + 1) % 2], jnp.concatenate(rows, axis=0), preferred_element_type=F32
            )
            sum_ref[m] = term + jnp.where(step > 1, sum_ref[m], 0.0)

    in_turn(step, 4, receive, multiply)

    @pl.when(step == 4)
    def _():
        low = lax.broadcasted_iota(jnp.int32, (16, 128), 1) < 64
        for m in range(3):
            for k in range(8):
                for t in range(4):
                    column = slice(128 * t, 128 * t + 128)
                    upper = sum_ref[m, 32 * k : 32 * k + 16, column]
                    lower = sum_ref[m, 32 * k + 16 : 32 * k + 32, column]
                    even = jnp.where(low, upper, pltpu.roll(lower, 64, 1))
                    odd = jnp.where(low, pltpu.roll(upper, 64, 1), lower)
                    out_ref[k, 2 * t, 16 * m : 16 * m + 16, :] = even.astype(BF16)
                    out_ref[k, 2 * t + 1, 16 * m : 16 * m + 16, :] = odd.astype(BF16)


def contract(m, w, other):
    behind = pl.BlockSpec((3, 8, 64, 512), lambda s: (0, jnp.maximum(s - 1, 0), 0, 0))
    return pl.pallas_call(
        contract_kernel,
        grid=(5,),
        in_specs=[
            pl.BlockSpec((128, 8, 256), lambda s: (0, 0, jnp.minimum(s, 3))),
            behind,
            behind,
        ],
        out_specs=whole((8, 8, 48, 128)),
        out_shape=jax.ShapeDtypeStruct((8, 8, 48, 128), BF16),
        scratch_shapes=[pltpu.VMEM((2, 256, 1024), BF16), pltpu.VMEM((3, 256, 512), F32)],
        compiler_params=params(),
        name="contract",
    )(m, w, other)


def total_kernel(parts_ref, out_ref):
    total = parts_ref[0:8].astype(F32).sum(axis=0)
    for s in range(1, 8):
        total = total + parts_ref[8 * s : 8 * s + 8].astype(F32).sum(axis=0)
    for m in range(3):
        out_ref[m, 0:16, :] = total[16 * m : 16 * m + 16, 0:64]
        out_ref[m, 16:32, :] = total[16 * m : 16 * m + 16, 64:128]


def total_of(parts):
    return pl.pallas_call(
        total_kernel,
        out_shape=jax.ShapeDtypeStruct((3, 32, 64), F32),
        compiler_params=pltpu.CompilerParams(vmem_limit_bytes=VMEM_LIMIT),
        name="total",
    )(parts)


def exchange(x, axis):
    return lax.all_to_all(x, axis, split_axis=0, concat_axis=0, tiled=True)


def on_device(r_pairs, w_tiles, virt_energy, energy_shift):
    w = w_tiles[0]
    energy, shift = virt_energy.reshape(4, 128), energy_shift.reshape(1, 1)
    cubes, later = lax.optimization_barrier((make_cubes(r_pairs[0], w, shift), w))
    other = lax.ppermute(later, "core", [(0, 1), (1, 0)])
    met = exchange(cubes, BA + COL)
    home = exchange(combine_at_owner(energy, shift, met), BA + COL)
    parts = contract(home, w, other).reshape(64, 48, 128)
    return total_of(exchange(parts, ("xl", "y") + COL))[None]


def solution(mesh):
    mesh = Mesh(mesh.devices.reshape(2, 4, 2, 2, 4), BA + COL)
    in_specs = (P(), P(None, None, BA, COL, None), P(), P())
    out_specs = P(None, None, BA, COL)
    return jax.shard_map(
        on_device, mesh=mesh, in_specs=in_specs, out_specs=out_specs, check_vma=False
    )
```
